256 devices in a mesh: dom: 16 (over z, core), sub: 16 (over y, x).
Axes of the slice: x: 4, y: 4, z: 8, core: 2. Of those that a mesh axis runs over, the one named last changes fastest.
Arguments:
- start_fields: float32 [4, 512, 128, 128], P(None, 'dom', 'sub'), may hold values from -6 to 6
- source: float32 [2, 512, 128, 128], P(None, 'dom', 'sub'), may hold values from -4 to 4
- labels: int32 [512, 128, 128], P('dom', 'sub'), may hold values from 0 to 15
- wavenumber2: float32 [16], replicated, may hold values from 0.05 to 0.4
- absorption: float32 [16], replicated, may hold values from 1.5 to 8
- design_weight: float32 [16], replicated, may hold values from 0.2 to 1.5
- pairs: int32 [16, 16, 1024], P('dom', 'sub'), may hold values from 0 to 1023, each once within a row
- block_index: int32 [16, 16], P('dom'), may hold values from 0 to 15
- blocks: bfloat16 [16, 16, 2, 1024, 1024], P('dom', 'sub'), may hold values from -0.103125 to 0.703125, as said below
Outputs:
- forward: float32 [2, 512, 128, 128], P(None, 'dom', 'sub')
- adjoint: float32 [2, 512, 128, 128], P(None, 'dom', 'sub')
The draws below stay inside these ranges and needn't reach their ends.
Inputs may be any that keep to these rules, and one draw needn't show every extreme that they name: `pairs`: each row is a one-to-one pairing of the 1024 points of a patch; the rows of the last subdomain are not read. `block_index`: several patches may use the same block. `blocks`: index 0 of the third dimension is a block's real part, index 1 its imaginary part.
All inputs are finite; a program needn't handle non-finite values.
Results may differ from the reference program's by a relative error of at most 0.0029.
Values may be sent and summed in bfloat16 or wider, within the bound.
A program may use at most 192 MiB of HBM per device.

```python
import math
import jax
import jax.numpy as jnp
from jax import lax

NXL = 32
PATCH = 1024
SWEEPS = 4
ITERS = 2
NMAT = 16
NZ = 128
SUBDOMAINS = 16
GROUP = 16
NX = 512
NY = 128


def draw_source(key, part):
    values = jnp.clip(jax.random.normal(key, (2, NX, NY, NZ), jnp.float32), -4.0, 4.0)
    return values


def draw_blocks(key, part):
    block_shape = (SUBDOMAINS, GROUP, 2, PATCH, PATCH)
    random_part = jnp.clip(jax.random.normal(key, block_shape, jnp.float32), -4.0, 4.0)
    row_index = lax.broadcasted_iota(jnp.int32, (PATCH, PATCH), 0)
    col_index = lax.broadcasted_iota(jnp.int32, (PATCH, PATCH), 1)
    identity_mask = jnp.where(row_index == col_index, 1.0, 0.0).astype(jnp.float32)
    diagonal = jnp.array([0.6, 0.3], jnp.float32).reshape(2, 1, 1) * identity_mask
    values = diagonal + random_part * (0.8 / math.sqrt(PATCH))
    return values.astype(jnp.bfloat16)


def touch_ends(values, stream_key, low, largest):
    index_at = [jax.random.randint(jax.random.fold_in(stream_key, axis), (), 0, length) for axis, length in enumerate(values.shape)]
    widest = values.shape.index(max(values.shape))
    next_to = index_at[:widest] + [(index_at[widest] + 1) % values.shape[widest]] + index_at[widest + 1:]
    return values.at[tuple(index_at)].set(low).at[tuple(next_to)].set(largest)


def level_of(own_key, extent, split, least, top_value):
    level, own = 1.0, jax.random.fold_in(own_key, 6)
    for dim, parts in split:
        steps = jnp.exp(jax.random.uniform(jax.random.fold_in(own, dim), (parts,), jnp.float32, least / len(split), top_value / len(split)))
        level = level * jnp.repeat(steps, extent[dim] // parts).reshape([-1 if axis == dim else 1 for axis in range(len(extent))])
    return level


def scatter_about(key, dims, deviation, most, pieces=(), held_as=jnp.bfloat16):
    gain = level_of(key, dims, pieces, -0.22, 0.18) if pieces else 1.0
    drawn = jax.random.normal(key, dims, jnp.float32) * deviation * gain
    return jnp.minimum(jnp.maximum(drawn, -most), most).astype(held_as)


def setup_inputs(seed: int = 0) -> dict:
    key_list = jax.random.split(jax.random.key(seed), 10)
    start_fields = scatter_about(key_list[0], (4, NX, NY, NZ), 1.0, 6.0, ((1, 16), (2, 16)), jnp.float32)
    source = draw_source(jax.random.fold_in(key_list[9], 71), 0)
    labels = touch_ends(jax.random.randint(key_list[2], (NX, NY, NZ), 0, NMAT), jax.random.fold_in(key_list[2], 1), 0, NMAT - 1).astype(jnp.int32)
    wavenumber2 = jnp.clip(jax.random.uniform(key_list[3], (NMAT,), jnp.float32, 0.05, 0.4), 0.05, 0.4)
    absorption = jnp.clip(jnp.exp(jax.random.uniform(key_list[4], (NMAT,), jnp.float32, math.log(1.5), math.log(8.0))), 1.5, 8.0)
    design_weight = jnp.clip(jax.random.uniform(key_list[5], (NMAT,), jnp.float32, 0.2, 1.5), 0.2, 1.5)
    pairs = jax.vmap(lambda own: jax.random.permutation(own, PATCH))(jax.random.split(key_list[6], SUBDOMAINS * GROUP)).reshape((SUBDOMAINS, GROUP, PATCH)).astype(jnp.int32)
    block_index = touch_ends(jax.random.randint(key_list[7], (SUBDOMAINS, GROUP), 0, GROUP), jax.random.fold_in(key_list[7], 1), 0, GROUP - 1).astype(jnp.int32)
    blocks = draw_blocks(jax.random.fold_in(key_list[9], 71), 0)
    return dict(start_fields=start_fields, source=source, labels=labels, wavenumber2=wavenumber2, absorption=absorption, design_weight=design_weight, pairs=pairs, block_index=block_index, blocks=blocks)


def coefficients(labels, source, wavenumber2, absorption, design_weight):
    wave_sq = wavenumber2[labels]
    damping = absorption[labels]
    weight = design_weight[labels]
    shifted = 6.0 - wave_sq
    modulus = shifted * shifted + damping * damping
    return jnp.stack([shifted / modulus, damping / modulus, source[0], source[1], weight])


def relax_step(fields, neighbours, coefficient_stack):
    recip_real = coefficient_stack[0]
    recip_imag = coefficient_stack[1]
    weight = coefficient_stack[4]
    forward_real = coefficient_stack[2] + neighbours[0]
    forward_imag = coefficient_stack[3] + neighbours[1]
    adjoint_real = weight * fields[0] + neighbours[2]
    adjoint_imag = weight * fields[1] + neighbours[3]
    return jnp.stack([recip_real * forward_real - recip_imag * forward_imag,
                      recip_real * forward_imag + recip_imag * forward_real,
                      recip_real * adjoint_real + recip_imag * adjoint_imag,
                      recip_real * adjoint_imag - recip_imag * adjoint_real])


def invert(order):
    return jnp.zeros((PATCH,), jnp.int32).at[order].set(jnp.arange(PATCH, dtype=jnp.int32))


def per_domain(items):
    domain_jump, domain_blocks, domain_index = items
    chosen = domain_blocks[domain_index].astype(jnp.float32)
    values = domain_jump.astype(jnp.float32)
    real_part = jnp.einsum("csq,spq->csp", values, chosen[:, 0], precision=lax.Precision.HIGHEST)
    imag_part = jnp.einsum("csq,spq->csp", values, chosen[:, 1], precision=lax.Precision.HIGHEST)
    return jnp.stack([real_part[0] - imag_part[1], real_part[1] + imag_part[0],
                      real_part[2] - imag_part[3], real_part[3] + imag_part[2]])


def reference(start_fields, source, labels, wavenumber2, absorption, design_weight, pairs, block_index, blocks):
    coefficient_stack = coefficients(labels, source, wavenumber2, absorption, design_weight)
    inverse = jax.vmap(jax.vmap(invert))(pairs)
    last_domain = (jnp.arange(SUBDOMAINS) == SUBDOMAINS - 1)[None, :, None, None]
    fields = start_fields
    for iteration in range(ITERS):
        blocked = fields.reshape(4, SUBDOMAINS, NXL, NY, NZ)
        left_trace = blocked[:, :, 0].reshape(4, SUBDOMAINS, GROUP, PATCH)
        right_trace = blocked[:, :, -1].reshape(4, SUBDOMAINS, GROUP, PATCH)
        following = jnp.concatenate([left_trace[:, 1:], jnp.zeros_like(left_trace[:, :1])], axis=1)
        facing = jnp.take_along_axis(following, jnp.broadcast_to(pairs[None], following.shape), axis=3)
        jump_data = (facing - right_trace).astype(jnp.bfloat16)
        moved = lax.map(per_domain, (jnp.moveaxis(jump_data, 1, 0), blocks, block_index))
        transmitted = jnp.moveaxis(moved, 0, 1)
        right_ghost = jnp.where(last_domain, 0.0, facing + transmitted)
        returned = jnp.take_along_axis(right_trace - transmitted, jnp.broadcast_to(inverse[None], following.shape), axis=3)
        left_ghost = jnp.concatenate([jnp.zeros_like(returned[:, :1]), returned[:, :-1]], axis=1)
        left_ghost = left_ghost.reshape(4, SUBDOMAINS, 1, NY, NZ)
        right_ghost = right_ghost.reshape(4, SUBDOMAINS, 1, NY, NZ)
        for sweep_index in range(SWEEPS):
            blocked = fields.reshape(4, SUBDOMAINS, NXL, NY, NZ)
            across = jnp.concatenate([left_ghost, blocked, right_ghost], axis=2)
            x_sum = (across[:, :, 2:] + across[:, :, :-2]).reshape(4, NX, NY, NZ)
            y_padded = jnp.pad(fields, ((0, 0), (0, 0), (1, 1), (0, 0)))
            z_padded = jnp.pad(fields, ((0, 0), (0, 0), (0, 0), (1, 1)))
            neighbours = x_sum + (y_padded[:, :, 2:] + y_padded[:, :, :-2]) + (z_padded[..., 2:] + z_padded[..., :-2])
            fields = relax_step(fields, neighbours, coefficient_stack)
    return fields[0:2], fields[2:4]
```

```python
import functools

import jax
import jax.numpy as jnp
from jax import lax
from jax.experimental import pallas as pl
from jax.experimental.pallas import tpu as pltpu
from jax.sharding import PartitionSpec as P

SWEEPS = 4
ITERS = 2
MESH = pl.DeviceIdType.MESH
F32 = jnp.float32
BF16 = jnp.bfloat16


def torus_offsets(nx, ny):
    offsets = [(dx, dy) for dy in range(ny) for dx in range(nx)]
    hops = lambda o: min(o[0], nx - o[0]) + min(o[1], ny - o[1])
    order = sorted(range(1, nx * ny), key=lambda i: -hops(offsets[i]))
    return offsets, order


def kernel(
    shape,
    pairs_s,
    owner_s,
    wave_s,
    absorb_s,
    design_s,
    pairs_h,
    fields_h,
    source_h,
    labels_h,
    blocks_h,
    forward_h,
    adjoint_h,
    pairs_v,
    own,
    beside,
    coef,
    labels,
    block,
    facing_in,
    jumps,
    stacked,
    outgoing,
    products,
    rows32,
    face,
    left_out,
    right_out,
    left_in,
    right_in,
    halo_out,
    halo_in,
    load_sem,
    trace_sem,
    jump_send,
    jump_recv,
    prod_send,
    prod_recv,
    ghost_send,
    ghost_recv,
    halo_send,
    halo_recv,
    store_sem,
):
    n_dom, n_sub, nx = shape
    ny = n_sub // nx
    layers = fields_h.shape[1]
    offsets, order = torus_offsets(nx, ny)
    me_d = lax.axis_index("dom")
    me_s = lax.axis_index("sub")
    my_x, my_y = lax.rem(me_s, nx), lax.div(me_s, nx)
    before_d, after_d = lax.rem(me_d + n_dom - 1, n_dom), lax.rem(me_d + 1, n_dom)
    before_s, after_s = lax.rem(me_s + n_sub - 1, n_sub), lax.rem(me_s + 1, n_sub)

    def member(slot):
        dx, dy = offsets[slot]
        return lax.rem(my_y + dy, ny) * nx + lax.rem(my_x + dx, nx)

    loads = [
        pltpu.make_async_copy(pairs_h, pairs_v, load_sem.at[0]),
        pltpu.make_async_copy(fields_h, own.at[0], load_sem.at[1]),
        pltpu.make_async_copy(labels_h, labels, load_sem.at[2]),
        pltpu.make_async_copy(source_h, coef.at[2:4, 0], load_sem.at[3]),
        pltpu.make_async_copy(blocks_h.at[0, 0], block, load_sem.at[4]),
    ]
    for load in loads:
        load.start()

    barrier = pltpu.get_barrier_semaphore()
    greeted = [(me_d, member(slot)) for slot in order]
    for dom in (before_d, after_d):
        for sub in (before_s, me_s, after_s):
            greeted.append((dom, sub))
    for device in greeted:
        pl.semaphore_signal(barrier, inc=1, device_id=device, device_id_type=MESH)

    row = lax.broadcasted_iota(jnp.int32, (8, 128), 0)
    lane = lax.broadcasted_iota(jnp.int32, (8, 128), 1)
    upper = row < 4
    even = lax.rem(row, 2) == 0
    not_first = jnp.where(me_d == 0, 0.0, 1.0).astype(F32)
    not_last = jnp.where(me_d == n_dom - 1, 0.0, 1.0).astype(F32)
    has_before = jnp.where(me_s == 0, 0.0, 1.0).astype(F32)
    has_after = jnp.where(me_s == n_sub - 1, 0.0, 1.0).astype(F32)
    beside_mask = jnp.where(upper, has_after, has_before)

    def roll4(value):
        return pltpu.roll(value, 4, 0)

    wave = jnp.zeros((8, 128), F32)
    absorb = jnp.zeros((8, 128), F32)
    weight_table = jnp.zeros((8, 128), F32)
    for m in range(16):
        wave = jnp.where(lane == m, wave_s[m], wave)
        absorb = jnp.where(lane == m, absorb_s[m], absorb)
        weight_table = jnp.where(lane == m, design_s[m], weight_table)
    shifted = 6.0 - wave
    modulus = shifted * shifted + absorb * absorb
    real_table = shifted / modulus
    imag_table = absorb / modulus

    def look(table, index):
        return jnp.take_along_axis(table, index, axis=1, mode="promise_in_bounds")

    position = row * 128 + lane

    def place(step, carry):
        for t in range(16):
            point = step * 16 + t
            carry = jnp.where(position == pairs_s[0, point], point, carry)
        return carry

    inverse = lax.fori_loop(0, 64, place, jnp.zeros((8, 128), jnp.int32))
    loads[0].wait()
    pairs = pairs_v[...]

    def gather_points(read_row, index):
        index_row = lax.shift_right_logical(index, 7)
        index_lane = lax.bitwise_and(index, 127)
        out = jnp.zeros((8, 128), F32)
        for r in range(8):
            source_row = jnp.broadcast_to(read_row(r), (8, 128))
            out = jnp.where(index_row == r, look(source_row, index_lane), out)
        return out

    pl.semaphore_wait(barrier, len(greeted))

    def trace_copy(it):
        return pltpu.make_async_remote_copy(
            src_ref=fields_h.at[:, 0] if it == 0 else own.at[0, :, 0],
            dst_ref=facing_in.at[it],
            send_sem=trace_sem.at[0, it],
            recv_sem=trace_sem.at[1, it],
            device_id=(before_d, me_s),
            device_id_type=MESH,
        )

    def jump_copy(it, slot):
        return pltpu.make_async_remote_copy(
            src_ref=jumps.at[it, 0],
            dst_ref=jumps.at[it, slot],
            send_sem=jump_send.at[it, slot],
            recv_sem=jump_recv.at[it, slot],
            device_id=(me_d, member(slot)),
            device_id_type=MESH,
        )

    def product_copy(it, slot):
        dx, dy = offsets[slot]
        back = lax.rem(my_y + ny - dy, ny) * nx + lax.rem(my_x + nx - dx, nx)
        return pltpu.make_async_remote_copy(
            src_ref=outgoing.at[it, slot],
            dst_ref=products.at[it, slot],
            send_sem=prod_send.at[it, slot],
            recv_sem=prod_recv.at[it, slot],
            device_id=(me_d, back),
            device_id_type=MESH,
        )

    def ghost_copies(it):
        copies = []
        for k, (src, dst, device) in enumerate(
            (
                (left_out, left_in.at[it, 0], (after_d, me_s)),
                (left_out, left_in.at[it, 1], (after_d, after_s)),
                (left_out, left_in.at[it, 2], (after_d, before_s)),
                (right_out, right_in.at[it, 0], (me_d, after_s)),
                (right_out, right_in.at[it, 1], (me_d, before_s)),
            )
        ):
            copies.append(
                pltpu.make_async_remote_copy(
                    src_ref=src.at[it],
                    dst_ref=dst,
                    send_sem=ghost_send.at[it, k],
                    recv_sem=ghost_recv.at[it, k],
                    device_id=device,
                    device_id_type=MESH,
                )
            )
        return copies

    def halo_copies(it):
        count = halo_out.shape[1] if it == 0 else 4
        copies = []
        for k, sub in enumerate((after_s, before_s)):
            copies.append(
                pltpu.make_async_remote_copy(
                    src_ref=halo_out.at[k, 0:count] if it == 0 else halo_out.at[k + 2, 0:count],
                    dst_ref=halo_in.at[k, 0:count] if it == 0 else halo_in.at[k + 2, 0:count],
                    send_sem=halo_send.at[it, k],
                    recv_sem=halo_recv.at[it, k],
                    device_id=(me_d, sub),
                    device_id_type=MESH,
                )
            )
        return copies

    half = layers // 2

    def pack_halo(it, item, read):
        base = 2 * it

        def step(k, carry):
            downs, ups = [], []
            for t in range(2):
                near = read(2 * k + t)
                far = roll4(read(half + 2 * k + t))
                downs.append(jnp.where(upper, far, near))
                ups.append(jnp.where(upper, near, far))
            halo_out[base, item, k] = jnp.concatenate(downs, 0).astype(BF16)
            halo_out[base + 1, item, k] = jnp.concatenate(ups, 0).astype(BF16)
            return carry

        lax.fori_loop(0, half // 2, step, 0, unroll=4)

    def unpack_halo(it, item, write):
        base = 2 * it

        def step(k, carry):
            down = halo_in[base, item, k].astype(F32)
            up = halo_in[base + 1, item, k].astype(F32)
            for t in range(2):
                d, u = down[8 * t : 8 * t + 8], up[8 * t : 8 * t + 8]
                write(2 * k + t, jnp.where(upper, u, d))
                write(half + 2 * k + t, roll4(jnp.where(upper, d, u)))
            return carry

        lax.fori_loop(0, half // 2, step, 0, unroll=2)

    def z_sum(v):
        low = jnp.where(lane == 0, 0.0, pltpu.roll(v, 1, 1))
        high = jnp.where(lane == 127, 0.0, pltpu.roll(v, 127, 1))
        return low + high

    def relax(cur, across, layer, tiles):
        sums = [[None] * 4 for _ in range(2)]
        for c in range(4):
            a, b = cur[0][c], cur[1][c]
            a_up, b_up = pltpu.roll(a, 1, 0), pltpu.roll(b, 1, 0)
            a_dn, b_dn = pltpu.roll(a, 7, 0), pltpu.roll(b, 7, 0)
            for t in tiles:
                v = (a, b)[t]
                mine_up, mine_dn = ((a_up, a_dn), (b_up, b_dn))[t]
                other_up, other_dn = ((b_up, b_dn), (a_up, a_dn))[t]
                y_sum = jnp.where(row == 0, other_up, mine_up) + jnp.where(
                    row == 7, other_dn, mine_dn
                )
                sums[t][c] = across[t][c] + y_sum + z_sum(v)
        results = []
        for t in tiles:
            rr, ri = coef[0, t, layer], coef[1, t, layer]
            w = coef[4, t, layer]
            fr = coef[2, t, layer] + sums[t][0]
            fi = coef[3, t, layer] + sums[t][1]
            ar = w * cur[t][0] + sums[t][2]
            ai = w * cur[t][1] + sums[t][3]
            results.append(
                (rr * fr - ri * fi, rr * fi + ri * fr, rr * ar + ri * ai, rr * ai - ri * ar)
            )
        return results

    buffers = (own, beside)

    def sweep_run(level, first, count, tiles):
        src, dst = level % 2, (level + 1) % 2

        def fetch(layer):
            return [[buffers[t][src, c, layer] for c in range(4)] for t in range(2)]

        values = [fetch(first + i) for i in range(-1, count + 1)]
        for i in range(count):
            low, cur, high = values[i], values[i + 1], values[i + 2]
            across = [[low[t][c] + high[t][c] for c in range(4)] for t in range(2)]
            results = relax(cur, across, first + i, tiles)
            for t, result in zip(tiles, results):
                for c in range(4):
                    buffers[t][dst, c, first + i] = result[c]

    def sweep_inside(level):
        tiles = (0, 1) if level < SWEEPS - 1 else (0,)
        first, last = level + 1, layers - 2 - level
        total = last - first + 1
        chunk = 4
        trips = total // chunk

        def step(k, carry):
            sweep_run(level, first + k * chunk, chunk, tiles)
            return carry

        lax.fori_loop(0, trips, step, 0)
        if total - trips * chunk:
            sweep_run(level, first + trips * chunk, total - trips * chunk, tiles)

    def sweep_end(level, ghosts, at_start):
        tiles = (0, 1) if level < SWEEPS - 1 else (0,)
        src, dst = level % 2, (level + 1) % 2
        count = level + 1
        span = range(0, count) if at_start else range(layers - count, layers)

        def fetch(layer):
            if layer < 0 or layer >= layers:
                return ghosts
            return [[buffers[t][src, c, layer] for c in range(4)] for t in range(2)]

        values = {layer: fetch(layer) for layer in range(span[0] - 1, span[-1] + 2)}
        for layer in span:
            low, cur, high = values[layer - 1], values[layer], values[layer + 1]
            across = [[low[t][c] + high[t][c] for c in range(4)] for t in range(2)]
            results = relax(cur, across, layer, tiles)
            for t, result in zip(tiles, results):
                for c in range(4):
                    buffers[t][dst, c, layer] = result[c]

    def coefficients_of(tile, mask=None, read=None):
        def step(layer, carry):
            lab = read(layer)
            rr, ri = look(real_table, lab), look(imag_table, lab)
            if mask is not None:
                rr, ri = rr * mask, ri * mask
            coef[0, tile, layer] = rr
            coef[1, tile, layer] = ri
            coef[4, tile, layer] = look(weight_table, lab)
            return carry

        lax.fori_loop(0, layers, step, 0, unroll=4)

    trace_copy(0).start()
    loads[1].wait()
    loads[2].wait()
    loads[3].wait()

    for it in range(ITERS):
        trace = trace_copy(it)
        if it == 0:
            pack_halo(0, 0, lambda l: own[0, 0, l])
            pack_halo(0, 1, lambda l: own[0, 1, l])
        trace.wait_recv()
        facing = []
        for c in range(4):
            taken = gather_points(lambda r: facing_in[it, c, r : r + 1, :], pairs)
            taken = taken * not_last
            facing.append(taken)
            face[c] = taken
            rows32[pl.ds(c, 8, stride=4), :] = taken - own[0, c, layers - 1]
        jumps[it, 0] = rows32[...].astype(BF16)
        for slot in order:
            jump_copy(it, slot).start()

        first_item = 2 if it == 0 else 0
        for c in range(first_item, 4):
            pack_halo(it, c, lambda l, c=c: own[0, c, l])
        if it == 0:
            pack_halo(0, 4, lambda l: coef[2, 0, l])
            pack_halo(0, 5, lambda l: coef[3, 0, l])
            pack_halo(0, 6, lambda l: labels[l].astype(F32))
        for copy in halo_copies(it):
            copy.start()
        if it == 0:
            coefficients_of(0, read=lambda l: labels[l])
            loads[4].wait()

        for slot in order:
            jump_copy(it, slot).wait_recv()
        for i in range(0, n_sub, 4):
            first = [jumps[it, i + t].astype(F32) for t in range(4)]
            for r in range(8):
                k, odd = r // 2, r % 2
                plain, turned = [], []
                for t in (0, 2):
                    a = first[t][8 * k : 8 * k + 8]
                    b = first[t + 1][8 * k : 8 * k + 8]
                    v = jnp.where(upper, roll4(a) if odd else a, b if odd else roll4(b))
                    plain.append(v)
                    turned.append(jnp.where(even, -pltpu.roll(v, 7, 0), pltpu.roll(v, 1, 0)))
                stacked[0, 4 * i : 4 * i + 16, r * 128 : r * 128 + 128] = jnp.concatenate(
                    plain, 0
                ).astype(BF16)
                stacked[1, 4 * i : 4 * i + 16, r * 128 : r * 128 + 128] = jnp.concatenate(
                    turned, 0
                ).astype(BF16)
        contract = (((1,), (1,)), ((), ()))
        total = lax.dot_general(
            stacked[0], block[0], contract, preferred_element_type=F32
        ) + lax.dot_general(stacked[1], block[1], contract, preferred_element_type=F32)
        for i in range(0, n_sub, 2):
            rows = total[4 * i : 4 * i + 8]
            evens, odds = [], []
            for k in range(4):
                a = rows[:, 256 * k : 256 * k + 128]
                b = rows[:, 256 * k + 128 : 256 * k + 256]
                evens.append(jnp.where(upper, a, roll4(b)))
                odds.append(jnp.where(upper, roll4(a), b))
            outgoing[it, i] = jnp.concatenate(evens, 0).astype(BF16)
            outgoing[it, i + 1] = jnp.concatenate(odds, 0).astype(BF16)
        for slot in order:
            product_copy(it, slot).start()
        products[it, 0] = outgoing[it, 0]

        for copy in halo_copies(it):
            copy.wait_recv()
        for c in range(4):
            def write_field(l, v, c=c):
                beside[0, c, l] = v * beside_mask

            unpack_halo(it, c, write_field)
        if it == 0:
            for c in range(2):
                def write_source(l, v, c=c):
                    coef[2 + c, 1, l] = v

                unpack_halo(0, 4 + c, write_source)

            def write_coef(l, v):
                lab = v.astype(jnp.int32)
                coef[0, 1, l] = look(real_table, lab) * beside_mask
                coef[1, 1, l] = look(imag_table, lab) * beside_mask
                coef[4, 1, l] = look(weight_table, lab)

            unpack_halo(0, 6, write_coef)
        for level in range(SWEEPS):
            sweep_inside(level)

        for slot in order:
            product_copy(it, slot).wait_recv()
        owner = owner_s[0, me_s]
        owner_dx = lax.rem(lax.rem(owner, nx) - my_x + nx, nx)
        owner_dy = lax.rem(lax.div(owner, nx) - my_y + ny, ny)
        rows32[...] = products[it, owner_dy * nx + owner_dx].astype(F32)
        right_own, back = [], []
        for c in range(4):
            moved = rows32[pl.ds(c, 8, stride=4), :]
            right = (face[c] + moved) * not_last
            right_own.append(right)
            right_out[it, c] = right
            face[c] = own[0, c, layers - 1] - moved
        for c in range(4):
            left_out[it, c] = gather_points(lambda r: face[c, r : r + 1, :], inverse)
        ghosts = ghost_copies(it)
        for copy in ghosts:
            copy.start()
        trace.wait_send()
        for copy in ghosts[3:]:
            copy.wait_recv()
        right_ghosts = [
            right_own,
            [jnp.where(upper, right_in[it, 1, c], right_in[it, 0, c]) for c in range(4)],
        ]
        for level in range(SWEEPS):
            sweep_end(level, right_ghosts, False)
        for copy in ghosts[:3]:
            copy.wait_recv()
        left_ghosts = [
            [left_in[it, 0, c] * not_first for c in range(4)],
            [
                jnp.where(upper, left_in[it, 2, c], left_in[it, 1, c]) * not_first
                for c in range(4)
            ],
        ]
        for level in range(SWEEPS):
            sweep_end(level, left_ghosts, True)
        if it + 1 < ITERS:
            trace_copy(it + 1).start()
        for slot in order:
            jump_copy(it, slot).wait_send()
            product_copy(it, slot).wait_send()
        for copy in ghosts + halo_copies(it):
            copy.wait_send()

    stores = [
        pltpu.make_async_copy(own.at[0, 0:2], forward_h, store_sem.at[0]),
        pltpu.make_async_copy(own.at[0, 2:4], adjoint_h, store_sem.at[1]),
    ]
    for store in stores:
        store.start()
    for store in stores:
        store.wait()


def solution(mesh):
    n_dom, n_sub = mesh.shape["dom"], mesh.shape["sub"]
    nx = 4 if n_sub % 4 == 0 and n_sub > 4 else 2

    def per_device(
        start_fields,
        source,
        labels,
        wavenumber2,
        absorption,
        design_weight,
        pairs,
        block_index,
        blocks,
    ):
        layers = labels.shape[0]
        points = pairs.shape[-1]
        slots = n_sub
        smem = pl.BlockSpec(memory_space=pltpu.SMEM)
        hbm = pl.BlockSpec(memory_space=pl.ANY)
        out = jax.ShapeDtypeStruct((2,) + labels.shape, F32)
        dma = pltpu.SemaphoreType.DMA
        return pl.pallas_call(
            functools.partial(kernel, (n_dom, n_sub, nx)),
            out_shape=(out, out),
            in_specs=[smem] * 5 + [hbm] * 5,
            out_specs=(hbm, hbm),
            scratch_shapes=[
                pltpu.VMEM((8, 128), jnp.int32),
                pltpu.VMEM((2, 4, layers, 8, 128), F32),
                pltpu.VMEM((2, 4, layers, 8, 128), F32),
                pltpu.VMEM((5, 2, layers, 8, 128), F32),
                pltpu.VMEM((layers, 8, 128), jnp.int32),
                pltpu.VMEM((2, points, points), BF16),
                pltpu.VMEM((ITERS, 4, 8, 128), F32),
                pltpu.VMEM((ITERS, slots, 32, 128), BF16),
                pltpu.VMEM((2, 4 * slots, points), BF16),
                pltpu.VMEM((ITERS, slots, 32, 128), BF16),
                pltpu.VMEM((ITERS, slots, 32, 128), BF16),
                pltpu.VMEM((32, 128), F32),
                pltpu.VMEM((4, 8, 128), F32),
                pltpu.VMEM((ITERS, 4, 8, 128), F32),
                pltpu.VMEM((ITERS, 4, 8, 128), F32),
                pltpu.VMEM((ITERS, 3, 4, 8, 128), F32),
                pltpu.VMEM((ITERS, 2, 4, 8, 128), F32),
                pltpu.VMEM((4, 7, layers // 4, 16, 128), BF16),
                pltpu.VMEM((4, 7, layers // 4, 16, 128), BF16),
                dma((5,)),
                dma((2, ITERS)),
                dma((ITERS, slots)),
                dma((ITERS, slots)),
                dma((ITERS, slots)),
                dma((ITERS, slots)),
                dma((ITERS, 5)),
                dma((ITERS, 5)),
                dma((ITERS, 2)),
                dma((ITERS, 2)),
                dma((2,)),
            ],
            compiler_params=pltpu.CompilerParams(
                collective_id=0, has_side_effects=True, vmem_limit_bytes=48 * 1024 * 1024
            ),
        )(
            pairs[0],
            block_index,
            wavenumber2,
            absorption,
            design_weight,
            pairs.reshape(8, 128),
            start_fields,
            source,
            labels,
            blocks,
        )

    placed = (
        P(None, "dom", "sub", None),
        P(None, "dom", "sub", None),
        P("dom", "sub", None),
        P(),
        P(),
        P(),
        P("dom", "sub", None),
        P("dom", None),
        P("dom", "sub", None, None, None),
    )
    return jax.shard_map(
        per_device,
        mesh=mesh,
        in_specs=placed,
        out_specs=(P(None, "dom", "sub", None), P(None, "dom", "sub", None)),
        check_vma=False,
    )
```

```python
import functools

import jax
import jax.numpy as jnp
from jax import lax
from jax.experimental import pallas as pl
from jax.experimental.pallas import tpu as pltpu
from jax.sharding import PartitionSpec as P

SWEEPS = 4
ITERS = 2
MESH = pl.DeviceIdType.MESH
F32 = jnp.float32
BF16 = jnp.bfloat16


def torus_offsets(nx, ny):
    offsets = [(dx, dy) for dy in range(ny) for dx in range(nx)]
    hops = lambda o: min(o[0], nx - o[0]) + min(o[1], ny - o[1])
    order = sorted(range(1, nx * ny), key=lambda i: -hops(offsets[i]))
    return offsets, order


def kernel(
    shape,
    pairs_flat_h,
    owner_h,
    wave_h,
    absorb_h,
    design_h,
    pairs_h,
    fields_h,
    source_h,
    labels_h,
    blocks_h,
    forward,
    adjoint,
    pairs_s,
    owner_s,
    wave_s,
    absorb_s,
    design_s,
    pairs_v,
    own,
    beside,
    coef,
    labels,
    block,
    facing_in,
    jumps,
    stacked,
    outgoing,
    products,
    rows32,
    face,
    left_out,
    right_out,
    left_in,
    right_in,
    halo_out,
    halo_in,
    load_sem,
    trace_sem,
    jump_send,
    jump_recv,
    prod_send,
    prod_recv,
    ghost_send,
    ghost_recv,
    halo_send,
    halo_recv,
):
    n_dom, n_sub, nx = shape
    ny = n_sub // nx
    layers = fields_h.shape[1]
    offsets, order = torus_offsets(nx, ny)
    me_d = lax.axis_index("dom")
    me_s = lax.axis_index("sub")
    my_x, my_y = lax.rem(me_s, nx), lax.div(me_s, nx)
    before_d, after_d = lax.rem(me_d + n_dom - 1, n_dom), lax.rem(me_d + 1, n_dom)
    before_s, after_s = lax.rem(me_s + n_sub - 1, n_sub), lax.rem(me_s + 1, n_sub)

    def member(slot):
        dx, dy = offsets[slot]
        return lax.rem(my_y + dy, ny) * nx + lax.rem(my_x + dx, nx)

    small_loads = [
        pltpu.make_async_copy(src, dst, load_sem.at[5 + k])
        for k, (src, dst) in enumerate(
            (
                (pairs_flat_h, pairs_s),
                (owner_h, owner_s),
                (wave_h, wave_s),
                (absorb_h, absorb_s),
                (design_h, design_s),
            )
        )
    ]
    for load in small_loads:
        load.start()
    loads = [
        pltpu.make_async_copy(pairs_h, pairs_v, load_sem.at[0]),
        pltpu.make_async_copy(fields_h, own.at[0], load_sem.at[1]),
        pltpu.make_async_copy(labels_h, labels, load_sem.at[2]),
        pltpu.make_async_copy(source_h, coef.at[2:4, 0], load_sem.at[3]),
        pltpu.make_async_copy(blocks_h.at[0, 0], block, load_sem.at[4]),
    ]
    for load in loads[:4]:
        load.start()

    barrier = pltpu.get_barrier_semaphore()
    greeted = [(me_d, member(slot)) for slot in order]
    for dom in (before_d, after_d):
        for sub in (before_s, me_s, after_s):
            greeted.append((dom, sub))
    for device in greeted:
        pl.semaphore_signal(barrier, inc=1, device_id=device, device_id_type=MESH)

    row = lax.broadcasted_iota(jnp.int32, (8, 128), 0)
    lane = lax.broadcasted_iota(jnp.int32, (8, 128), 1)
    upper = row < 4
    even = lax.rem(row, 2) == 0
    not_first = jnp.where(me_d == 0, 0.0, 1.0).astype(F32)
    not_last = jnp.where(me_d == n_dom - 1, 0.0, 1.0).astype(F32)
    has_before = jnp.where(me_s == 0, 0.0, 1.0).astype(F32)
    has_after = jnp.where(me_s == n_sub - 1, 0.0, 1.0).astype(F32)
    beside_mask = jnp.where(upper, has_after, has_before)

    def roll4(value):
        return pltpu.roll(value, 4, 0)

    def trace_copy(it):
        return pltpu.make_async_remote_copy(
            src_ref=fields_h.at[:, 0] if it == 0 else own.at[0, :, 0],
            dst_ref=facing_in.at[it],
            send_sem=trace_sem.at[0, it],
            recv_sem=trace_sem.at[1, it],
            device_id=(before_d, me_s),
            device_id_type=MESH,
        )

    def jump_copy(it, slot):
        return pltpu.make_async_remote_copy(
            src_ref=jumps.at[it, 0],
            dst_ref=jumps.at[it, slot],
            send_sem=jump_send.at[it, slot],
            recv_sem=jump_recv.at[it, slot],
            device_id=(me_d, member(slot)),
            device_id_type=MESH,
        )

    def product_copy(it, slot, part):
        dx, dy = offsets[slot]
        back = lax.rem(my_y + ny - dy, ny) * nx + lax.rem(my_x + nx - dx, nx)
        rows = pl.ds(16 * part, 16)
        return pltpu.make_async_remote_copy(
            src_ref=outgoing.at[it, slot, rows],
            dst_ref=products.at[it, slot, rows],
            send_sem=prod_send.at[it, slot, part],
            recv_sem=prod_recv.at[it, slot, part],
            device_id=(me_d, back),
            device_id_type=MESH,
        )

    def ghost_copies(it):
        copies = []
        for k, (src, dst, device) in enumerate(
            (
                (left_out, left_in.at[it, 0], (after_d, me_s)),
                (left_out, left_in.at[it, 1], (after_d, after_s)),
                (left_out, left_in.at[it, 2], (after_d, before_s)),
                (right_out, right_in.at[it, 0], (me_d, after_s)),
                (right_out, right_in.at[it, 1], (me_d, before_s)),
            )
        ):
            copies.append(
                pltpu.make_async_remote_copy(
                    src_ref=src.at[it],
                    dst_ref=dst,
                    send_sem=ghost_send.at[it, k],
                    recv_sem=ghost_recv.at[it, k],
                    device_id=device,
                    device_id_type=MESH,
                )
            )
        return copies

    def halo_copies(it, second=False):
        groups = halo_out.shape[2]
        if it == 0:
            items, span = ((4, 3) if second else (0, 4)), (0, groups)
        else:
            items, span = (0, 4), ((0, 2) if second else (2, groups - 2))
        copies = []
        for k, sub in enumerate((after_s, before_s)):
            part = (2 * it + k, pl.ds(*items), pl.ds(*span))
            copies.append(
                pltpu.make_async_remote_copy(
                    src_ref=halo_out.at[part],
                    dst_ref=halo_in.at[part],
                    send_sem=halo_send.at[2 * it + second, k],
                    recv_sem=halo_recv.at[2 * it + second, k],
                    device_id=(me_d, sub),
                    device_id_type=MESH,
                )
            )
        return copies

    half = layers // 2

    def pack_halo(it, item, read, start=0, stop=None):
        base = 2 * it

        def step(k, carry):
            downs, ups = [], []
            for t in range(2):
                near = read(2 * k + t)
                far = roll4(read(layers - 1 - 2 * k - t))
                downs.append(jnp.where(upper, far, near))
                ups.append(jnp.where(upper, near, far))
            halo_out[base, item, k] = jnp.concatenate(downs, 0).astype(BF16)
            halo_out[base + 1, item, k] = jnp.concatenate(ups, 0).astype(BF16)
            return carry

        lax.fori_loop(start, stop or half // 2, step, 0, unroll=2)

    def unpack_halo(it, item, write, start=0, stop=None):
        base = 2 * it

        def step(k, carry):
            down = halo_in[base, item, k].astype(F32)
            up = halo_in[base + 1, item, k].astype(F32)
            for t in range(2):
                d, u = down[8 * t : 8 * t + 8], up[8 * t : 8 * t + 8]
                write(2 * k + t, jnp.where(upper, u, d))
                write(layers - 1 - 2 * k - t, roll4(jnp.where(upper, d, u)))
            return carry

        lax.fori_loop(start, stop or half // 2, step, 0, unroll=2)

    def unpack_fields(it, start, stop):
        for c in range(4):
            def write_field(l, v, c=c):
                beside[0, c, l] = v * beside_mask

            unpack_halo(it, c, write_field, start, stop)

    def z_sum(v):
        low = jnp.where(lane == 0, 0.0, pltpu.roll(v, 1, 1))
        high = jnp.where(lane == 127, 0.0, pltpu.roll(v, 127, 1))
        return low + high

    def relax(cur, across, layer, tiles):
        sums = [[None] * 4 for _ in range(2)]
        for c in range(4):
            a, b = cur[0][c], cur[1][c]
            a_up, b_up = pltpu.roll(a, 1, 0), pltpu.roll(b, 1, 0)
            a_dn, b_dn = pltpu.roll(a, 7, 0), pltpu.roll(b, 7, 0)
            for t in tiles:
                v = (a, b)[t]
                mine_up, mine_dn = ((a_up, a_dn), (b_up, b_dn))[t]
                other_up, other_dn = ((b_up, b_dn), (a_up, a_dn))[t]
                y_sum = jnp.where(row == 0, other_up, mine_up) + jnp.where(
                    row == 7, other_dn, mine_dn
                )
                sums[t][c] = across[t][c] + y_sum + z_sum(v)
        results = []
        for t in tiles:
            rr, ri = coef[0, t, layer], coef[1, t, layer]
            w = coef[4, t, layer]
            fr = coef[2, t, layer] + sums[t][0]
            fi = coef[3, t, layer] + sums[t][1]
            ar = w * cur[t][0] + sums[t][2]
            ai = w * cur[t][1] + sums[t][3]
            results.append(
                (rr * fr - ri * fi, rr * fi + ri * fr, rr * ar + ri * ai, rr * ai - ri * ar)
            )
        return results

    buffers = (own, beside)

    def put(level, final, t, c, layer, value):
        if final and level == SWEEPS - 1:
            (forward, adjoint)[c // 2][c % 2, layer] = value
        else:
            buffers[t][(level + 1) % 2, c, layer] = value

    def sweep_run(level, first, count, tiles, final):
        src = level % 2

        def fetch(layer):
            return [[buffers[t][src, c, layer] for c in range(4)] for t in range(2)]

        values = [fetch(first + i) for i in range(-1, count + 1)]
        for i in range(count):
            low, cur, high = values[i], values[i + 1], values[i + 2]
            across = [[low[t][c] + high[t][c] for c in range(4)] for t in range(2)]
            results = relax(cur, across, first + i, tiles)
            for t, result in zip(tiles, results):
                for c in range(4):
                    put(level, final, t, c, first + i, result[c])

    def sweep_inside(level, final):
        tiles = (0, 1) if level < SWEEPS - 1 else (0,)
        first, last = level + 1, layers - 2 - level
        total = last - first + 1
        trips = 2
        chunk = total // trips

        def step(k, carry):
            sweep_run(level, first + k * chunk, chunk, tiles, final)
            return carry

        lax.fori_loop(0, trips, step, 0)

    def sweep_end(level, ghosts, at_start, final):
        tiles = (0, 1) if level < SWEEPS - 1 else (0,)
        src = level % 2
        count = level + 1
        span = range(0, count) if at_start else range(layers - count, layers)

        def fetch(layer):
            if layer < 0 or layer >= layers:
                return ghosts
            return [[buffers[t][src, c, layer] for c in range(4)] for t in range(2)]

        values = {layer: fetch(layer) for layer in range(span[0] - 1, span[-1] + 2)}
        for layer in span:
            low, cur, high = values[layer - 1], values[layer], values[layer + 1]
            across = [[low[t][c] + high[t][c] for c in range(4)] for t in range(2)]
            results = relax(cur, across, layer, tiles)
            for t, result in zip(tiles, results):
                for c in range(4):
                    put(level, final, t, c, layer, result[c])

    def coefficients_of(tile, mask=None, read=None):
        def step(layer, carry):
            lab = read(layer)
            rr, ri = look(real_table, lab), look(imag_table, lab)
            if mask is not None:
                rr, ri = rr * mask, ri * mask
            coef[0, tile, layer] = rr
            coef[1, tile, layer] = ri
            coef[4, tile, layer] = look(weight_table, lab)
            return carry

        lax.fori_loop(0, layers, step, 0, unroll=4)

    pl.semaphore_wait(barrier, len(greeted))
    trace_copy(0).start()
    for load in loads[1:4]:
        load.wait()
    loads[4].start()
    pack_halo(0, 4, lambda l: coef[2, 0, l])
    pack_halo(0, 5, lambda l: coef[3, 0, l])
    pack_halo(0, 6, lambda l: labels[l].astype(F32))
    for copy in halo_copies(0, True):
        copy.start()
    for c in range(4):
        pack_halo(0, c, lambda l, c=c: own[0, c, l])
    for load in small_loads:
        load.wait()

    wave = jnp.zeros((8, 128), F32)
    absorb = jnp.zeros((8, 128), F32)
    weight_table = jnp.zeros((8, 128), F32)
    for m in range(16):
        wave = jnp.where(lane == m, wave_s[m], wave)
        absorb = jnp.where(lane == m, absorb_s[m], absorb)
        weight_table = jnp.where(lane == m, design_s[m], weight_table)
    shifted = 6.0 - wave
    modulus = shifted * shifted + absorb * absorb
    real_table = shifted / modulus
    imag_table = absorb / modulus

    def look(table, index):
        return jnp.take_along_axis(table, index, axis=1, mode="promise_in_bounds")

    position = row * 128 + lane

    def place(step, carry):
        for t in range(16):
            point = step * 16 + t
            carry = jnp.where(position == pairs_s[0, point], point, carry)
        return carry

    loads[0].wait()
    pairs = pairs_v[...]

    def gather_points(read_row, index):
        index_row = lax.shift_right_logical(index, 7)
        index_lane = lax.bitwise_and(index, 127)
        out = jnp.zeros((8, 128), F32)
        for r in range(8):
            source_row = jnp.broadcast_to(read_row(r), (8, 128))
            out = jnp.where(index_row == r, look(source_row, index_lane), out)
        return out

    for it in range(ITERS):
        trace = trace_copy(it)
        trace.wait_recv()
        facing = []
        for c in range(4):
            taken = gather_points(lambda r: facing_in[it, c, r : r + 1, :], pairs)
            taken = taken * not_last
            facing.append(taken)
            face[c] = taken
            rows32[pl.ds(c, 8, stride=4), :] = taken - own[0, c, layers - 1]
        jumps[it, 0] = rows32[...].astype(BF16)
        for slot in order:
            jump_copy(it, slot).start()

        if it == 0:
            for copy in halo_copies(0):
                copy.start()
            coefficients_of(0, read=lambda l: labels[l])
            inverse = lax.fori_loop(0, 64, place, jnp.zeros((8, 128), jnp.int32))
            loads[4].wait()
        else:
            for c in range(4):
                pack_halo(it, c, lambda l, c=c: own[0, c, l], 0, 2)
            for copy in halo_copies(it, True):
                copy.start()
            for copy in halo_copies(it):
                copy.wait_recv()
            unpack_fields(it, 2, half // 2)
        for slot in order:
            jump_copy(it, slot).wait_recv()
        for i in range(0, n_sub, 4):
            first = [jumps[it, i + t].astype(F32) for t in range(4)]
            for r in range(8):
                k, odd = r // 2, r % 2
                plain, turned = [], []
                for t in (0, 2):
                    a = first[t][8 * k : 8 * k + 8]
                    b = first[t + 1][8 * k : 8 * k + 8]
                    v = jnp.where(upper, roll4(a) if odd else a, b if odd else roll4(b))
                    plain.append(v)
                    turned.append(jnp.where(even, -pltpu.roll(v, 7, 0), pltpu.roll(v, 1, 0)))
                stacked[0, 4 * i : 4 * i + 16, r * 128 : r * 128 + 128] = jnp.concatenate(
                    plain, 0
                ).astype(BF16)
                stacked[1, 4 * i : 4 * i + 16, r * 128 : r * 128 + 128] = jnp.concatenate(
                    turned, 0
                ).astype(BF16)
        contract = (((1,), (1,)), ((), ()))
        width = 512
        for part in range(2):
            span = pl.ds(width * part, width)
            total = lax.dot_general(
                stacked[0], block[0, span, :], contract, preferred_element_type=F32
            ) + lax.dot_general(
                stacked[1], block[1, span, :], contract, preferred_element_type=F32
            )
            for i in range(0, n_sub, 2):
                rows = total[4 * i : 4 * i + 8]
                evens, odds = [], []
                for k in range(2):
                    a = rows[:, 256 * k : 256 * k + 128]
                    b = rows[:, 256 * k + 128 : 256 * k + 256]
                    evens.append(jnp.where(upper, a, roll4(b)))
                    odds.append(jnp.where(upper, roll4(a), b))
                here = slice(16 * part, 16 * part + 16)
                outgoing[it, i, here] = jnp.concatenate(evens, 0).astype(BF16)
                outgoing[it, i + 1, here] = jnp.concatenate(odds, 0).astype(BF16)
            for slot in order:
                product_copy(it, slot, part).start()
        products[it, 0] = outgoing[it, 0]

        if it == 0:
            for copy in halo_copies(it, True) + halo_copies(it):
                copy.wait_recv()
            unpack_fields(it, 0, half // 2)
            for c in range(2):
                def write_source(l, v, c=c):
                    coef[2 + c, 1, l] = v

                unpack_halo(0, 4 + c, write_source)

            def write_coef(l, v):
                lab = v.astype(jnp.int32)
                coef[0, 1, l] = look(real_table, lab) * beside_mask
                coef[1, 1, l] = look(imag_table, lab) * beside_mask
                coef[4, 1, l] = look(weight_table, lab)

            unpack_halo(0, 6, write_coef)
        else:
            for copy in halo_copies(it, True):
                copy.wait_recv()
            unpack_fields(it, 0, 2)
        final = it == ITERS - 1
        for level in range(SWEEPS):
            sweep_inside(level, final)
        if not final:
            for c in range(4):
                pack_halo(it + 1, c, lambda l, c=c: own[0, c, l], 2)

        for slot in order:
            product_copy(it, slot, 0).wait_recv()
            product_copy(it, slot, 1).wait_recv()
        owner = owner_s[0, me_s]
        owner_dx = lax.rem(lax.rem(owner, nx) - my_x + nx, nx)
        owner_dy = lax.rem(lax.div(owner, nx) - my_y + ny, ny)
        rows32[...] = products[it, owner_dy * nx + owner_dx].astype(F32)
        right_own, back = [], []
        for c in range(4):
            moved = rows32[pl.ds(c, 8, stride=4), :]
            right = (face[c] + moved) * not_last
            right_own.append(right)
            right_out[it, c] = right
            face[c] = own[0, c, layers - 1] - moved
        for c in range(4):
            left_out[it, c] = gather_points(lambda r: face[c, r : r + 1, :], inverse)
        ghosts = ghost_copies(it)
        for copy in ghosts:
            copy.start()
        if not final:
            for copy in halo_copies(it + 1):
                copy.start()
        trace.wait_send()
        for copy in ghosts[:3]:
            copy.wait_recv()
        if final:
            for copy in ghosts[3:]:
                copy.wait_recv()
        left_ghosts = [
            [left_in[it, 0, c] * not_first for c in range(4)],
            [
                jnp.where(upper, left_in[it, 2, c], left_in[it, 1, c]) * not_first
                for c in range(4)
            ],
        ]
        if final:
            for level in range(SWEEPS):
                sweep_end(level, left_ghosts, True, final)
                if level == 0:
                    right_ghosts = [
                        right_own,
                        [
                            jnp.where(upper, right_in[it, 1, c], right_in[it, 0, c])
                            for c in range(4)
                        ],
                    ]
                sweep_end(level, right_ghosts, False, final)
        else:
            for level in range(SWEEPS):
                sweep_end(level, left_ghosts, True, final)
            trace_copy(it + 1).start()
            for copy in ghosts[3:]:
                copy.wait_recv()
            right_ghosts = [
                right_own,
                [jnp.where(upper, right_in[it, 1, c], right_in[it, 0, c]) for c in range(4)],
            ]
            for level in range(SWEEPS):
                sweep_end(level, right_ghosts, False, final)

    for it in range(ITERS):
        for slot in order:
            jump_copy(it, slot).wait_send()
            product_copy(it, slot, 0).wait_send()
            product_copy(it, slot, 1).wait_send()
        for copy in ghost_copies(it) + halo_copies(it) + halo_copies(it, True):
            copy.wait_send()


def store_kernel(forward_v, adjoint_v, forward_h, adjoint_h, sem):
    copies = [
        pltpu.make_async_copy(forward_v, forward_h, sem.at[0]),
        pltpu.make_async_copy(adjoint_v, adjoint_h, sem.at[1]),
    ]
    for copy in copies:
        copy.start()
    for copy in copies:
        copy.wait()


def solution(mesh):
    n_dom, n_sub = mesh.shape["dom"], mesh.shape["sub"]
    nx = 4 if n_sub % 4 == 0 and n_sub > 4 else 2

    def per_device(
        start_fields,
        source,
        labels,
        wavenumber2,
        absorption,
        design_weight,
        pairs,
        block_index,
        blocks,
    ):
        layers = labels.shape[0]
        points = pairs.shape[-1]
        slots = n_sub
        hbm = pl.BlockSpec(memory_space=pltpu.HBM)
        vmem = pl.BlockSpec(memory_space=pltpu.VMEM)
        out = jax.ShapeDtypeStruct((2,) + labels.shape, F32)
        dma = pltpu.SemaphoreType.DMA
        operands = [
            pltpu.with_memory_space_constraint(operand, pltpu.HBM)
            for operand in (
                pairs[0],
                block_index,
                wavenumber2,
                absorption,
                design_weight,
                pairs.reshape(8, 128),
                start_fields,
                source,
                labels,
                blocks,
            )
        ]
        results = pl.pallas_call(
            functools.partial(kernel, (n_dom, n_sub, nx)),
            out_shape=(out, out),
            in_specs=[hbm] * 10,
            out_specs=(vmem, vmem),
            scratch_shapes=[
                pltpu.SMEM((1, points), jnp.int32),
                pltpu.SMEM(block_index.shape, jnp.int32),
                pltpu.SMEM(wavenumber2.shape, F32),
                pltpu.SMEM(absorption.shape, F32),
                pltpu.SMEM(design_weight.shape, F32),
                pltpu.VMEM((8, 128), jnp.int32),
                pltpu.VMEM((2, 4, layers, 8, 128), F32),
                pltpu.VMEM((2, 4, layers, 8, 128), F32),
                pltpu.VMEM((5, 2, layers, 8, 128), F32),
                pltpu.VMEM((layers, 8, 128), jnp.int32),
                pltpu.VMEM((2, points, points), BF16),
                pltpu.VMEM((ITERS, 4, 8, 128), F32),
                pltpu.VMEM((ITERS, slots, 32, 128), BF16),
                pltpu.VMEM((2, 4 * slots, points), BF16),
                pltpu.VMEM((ITERS, slots, 32, 128), BF16),
                pltpu.VMEM((ITERS, slots, 32, 128), BF16),
                pltpu.VMEM((32, 128), F32),
                pltpu.VMEM((4, 8, 128), F32),
                pltpu.VMEM((ITERS, 4, 8, 128), F32),
                pltpu.VMEM((ITERS, 4, 8, 128), F32),
                pltpu.VMEM((ITERS, 3, 4, 8, 128), F32),
                pltpu.VMEM((ITERS, 2, 4, 8, 128), F32),
                pltpu.VMEM((4, 7, layers // 4, 16, 128), BF16),
                pltpu.VMEM((4, 7, layers // 4, 16, 128), BF16),
                dma((10,)),
                dma((2, ITERS)),
                dma((ITERS, slots)),
                dma((ITERS, slots)),
                dma((ITERS, slots, 2)),
                dma((ITERS, slots, 2)),
                dma((ITERS, 5)),
                dma((ITERS, 5)),
                dma((2 * ITERS, 2)),
                dma((2 * ITERS, 2)),
            ],
            compiler_params=pltpu.CompilerParams(
                collective_id=0, has_side_effects=True, vmem_limit_bytes=20 * 1024 * 1024
            ),
        )(*operands)
        return pl.pallas_call(
            store_kernel,
            out_shape=(out, out),
            in_specs=[vmem, vmem],
            out_specs=(hbm, hbm),
            scratch_shapes=[dma((2,))],
            compiler_params=pltpu.CompilerParams(vmem_limit_bytes=4 * 1024 * 1024),
        )(*results)

    placed = (
        P(None, "dom", "sub", None),
        P(None, "dom", "sub", None),
        P("dom", "sub", None),
        P(),
        P(),
        P(),
        P("dom", "sub", None),
        P("dom", None),
        P("dom", "sub", None, None, None),
    )
    return jax.shard_map(
        per_device,
        mesh=mesh,
        in_specs=placed,
        out_specs=(P(None, "dom", "sub", None), P(None, "dom", "sub", None)),
        check_vma=False,
    )
```

```python
import functools

import jax
import jax.numpy as jnp
from jax import lax
from jax.experimental import pallas as pl
from jax.experimental.pallas import tpu as pltpu
from jax.sharding import PartitionSpec as P

SWEEPS = 4
ITERS = 2
MESH = pl.DeviceIdType.MESH
F32 = jnp.float32
BF16 = jnp.bfloat16


def torus_offsets(nx, ny):
    offsets = [(dx, dy) for dy in range(ny) for dx in range(nx)]
    hops = lambda o: min(o[0], nx - o[0]) + min(o[1], ny - o[1])
    order = sorted(range(1, nx * ny), key=lambda i: -hops(offsets[i]))
    return offsets, order


def kernel(
    shape,
    pairs_flat_h,
    owner_h,
    wave_h,
    absorb_h,
    design_h,
    pairs_h,
    fields_h,
    source_h,
    labels_h,
    blocks_h,
    forward,
    adjoint,
    pairs_s,
    owner_s,
    wave_s,
    absorb_s,
    design_s,
    pairs_v,
    own,
    beside,
    coef,
    labels,
    block,
    facing_in,
    jumps,
    stacked,
    outgoing,
    products,
    rows32,
    face,
    left_out,
    left_in,
    side_out,
    side_in,
    inv_out,
    inv_in,
    halo_out,
    halo_in,
    load_sem,
    trace_sem,
    jump_send,
    jump_recv,
    prod_send,
    prod_recv,
    ghost_send,
    ghost_recv,
    side_send,
    side_recv,
    inv_send,
    inv_recv,
    halo_send,
    halo_recv,
    nxt,
    nxt_coef,
    nxt_out,
    nxt_send,
    nxt_recv,
):
    n_dom, n_sub, nx = shape
    ny = n_sub // nx
    layers = fields_h.shape[1]
    offsets, order = torus_offsets(nx, ny)
    me_d = lax.axis_index("dom")
    me_s = lax.axis_index("sub")
    my_x, my_y = lax.rem(me_s, nx), lax.div(me_s, nx)
    before_d, after_d = lax.rem(me_d + n_dom - 1, n_dom), lax.rem(me_d + 1, n_dom)
    before_s, after_s = lax.rem(me_s + n_sub - 1, n_sub), lax.rem(me_s + 1, n_sub)

    def member(slot):
        dx, dy = offsets[slot]
        return lax.rem(my_y + dy, ny) * nx + lax.rem(my_x + dx, nx)

    barrier = pltpu.get_barrier_semaphore()
    greeted = [(me_d, member(slot)) for slot in order]
    greeted += [(before_d, me_s), (after_d, me_s)]
    for device in greeted:
        pl.semaphore_signal(barrier, inc=1, device_id=device, device_id_type=MESH)

    small_loads = [
        pltpu.make_async_copy(src, dst, load_sem.at[5 + k])
        for k, (src, dst) in enumerate(
            (
                (pairs_flat_h, pairs_s),
                (owner_h, owner_s),
                (wave_h, wave_s),
                (absorb_h, absorb_s),
                (design_h, design_s),
            )
        )
    ]
    for load in small_loads:
        load.start()
    loads = [
        pltpu.make_async_copy(pairs_h, pairs_v, load_sem.at[0]),
        pltpu.make_async_copy(fields_h, own.at[0], load_sem.at[1]),
        pltpu.make_async_copy(labels_h, labels, load_sem.at[2]),
        pltpu.make_async_copy(source_h, coef.at[2:4, 0], load_sem.at[3]),
        pltpu.make_async_copy(blocks_h.at[0, 0], block, load_sem.at[4]),
    ]
    for load in loads[:4]:
        load.start()

    row = lax.broadcasted_iota(jnp.int32, (8, 128), 0)
    lane = lax.broadcasted_iota(jnp.int32, (8, 128), 1)
    upper = row < 4
    even = lax.rem(row, 2) == 0
    not_first = jnp.where(me_d == 0, 0.0, 1.0).astype(F32)
    not_last = jnp.where(me_d == n_dom - 1, 0.0, 1.0).astype(F32)
    has_before = jnp.where(me_s == 0, 0.0, 1.0).astype(F32)
    has_after = jnp.where(me_s == n_sub - 1, 0.0, 1.0).astype(F32)
    beside_mask = jnp.where(upper, has_after, has_before)

    def roll4(value):
        return pltpu.roll(value, 4, 0)

    depth = nxt.shape[3]

    def trace_copy():
        return pltpu.make_async_remote_copy(
            src_ref=fields_h.at[:, 0],
            dst_ref=facing_in,
            send_sem=trace_sem.at[0],
            recv_sem=trace_sem.at[1],
            device_id=(before_d, me_s),
            device_id_type=MESH,
        )

    def next_copies():
        copies = []
        for k, (src, dst) in enumerate(
            (
                (fields_h.at[:, 0:depth], nxt.at[0, 0]),
                (coef.at[:, 0, 0 : depth - 1], nxt_coef.at[:, 0]),
                (nxt_out, nxt.at[0, 1]),
                (coef.at[:, 1, 0 : depth - 1], nxt_coef.at[:, 1]),
            )
        ):
            copies.append(
                pltpu.make_async_remote_copy(
                    src_ref=src,
                    dst_ref=dst,
                    send_sem=nxt_send.at[k],
                    recv_sem=nxt_recv.at[k],
                    device_id=(before_d, me_s),
                    device_id_type=MESH,
                )
            )
        return copies

    def source_of(slot):
        dx, dy = offsets[slot]
        return lax.rem(my_y + ny - dy, ny) * nx + lax.rem(my_x + nx - dx, nx)

    def slot_of(member_index):
        dx = lax.rem(lax.rem(member_index, nx) - my_x + nx, nx)
        dy = lax.rem(lax.div(member_index, nx) - my_y + ny, ny)
        return dy * nx + dx

    def jump_copy(it, slot):
        return pltpu.make_async_remote_copy(
            src_ref=jumps.at[it, 0],
            dst_ref=jumps.at[it, slot],
            send_sem=jump_send.at[it, slot],
            recv_sem=jump_recv.at[it, slot],
            device_id=(me_d, member(slot)),
            device_id_type=MESH,
        )

    def product_copy(it, slot, part):
        back = source_of(slot)
        rows = pl.ds(16 * part, 16)
        return pltpu.make_async_remote_copy(
            src_ref=outgoing.at[it, pl.ds(back, 3), rows],
            dst_ref=products.at[it, slot, :, rows],
            send_sem=prod_send.at[it, slot, part],
            recv_sem=prod_recv.at[it, slot, part],
            device_id=(me_d, back),
            device_id_type=MESH,
        )

    def ghost_copy(it):
        return pltpu.make_async_remote_copy(
            src_ref=left_out.at[it],
            dst_ref=left_in.at[it],
            send_sem=ghost_send.at[it],
            recv_sem=ghost_recv.at[it],
            device_id=(after_d, me_s),
            device_id_type=MESH,
        )

    def beside_copies(src, dst, send_sem, recv_sem):
        return [
            pltpu.make_async_remote_copy(
                src_ref=src,
                dst_ref=dst.at[k],
                send_sem=send_sem.at[k],
                recv_sem=recv_sem.at[k],
                device_id=(me_d, sub),
                device_id_type=MESH,
            )
            for k, sub in enumerate((after_s, before_s))
        ]

    def side_copies(it):
        return beside_copies(side_out.at[it], side_in.at[it], side_send.at[it], side_recv.at[it])

    def inverse_copies():
        return beside_copies(inv_out, inv_in, inv_send, inv_recv)

    def halo_copies(it, second=False):
        groups = halo_out.shape[2]
        if it == 0:
            items, span = ((4, 3) if second else (0, 4)), (0, groups)
        else:
            items, span = (0, 4), ((0, 2) if second else (2, groups - 2))
        copies = []
        for k, sub in enumerate((after_s, before_s)):
            part = (2 * it + k, pl.ds(*items), pl.ds(*span))
            copies.append(
                pltpu.make_async_remote_copy(
                    src_ref=halo_out.at[part],
                    dst_ref=halo_in.at[part],
                    send_sem=halo_send.at[2 * it + second, k],
                    recv_sem=halo_recv.at[2 * it + second, k],
                    device_id=(me_d, sub),
                    device_id_type=MESH,
                )
            )
        return copies

    half = layers // 2

    def pack_halo(it, item, read, start=0, stop=None):
        base = 2 * it

        def step(k, carry):
            downs, ups = [], []
            for t in range(2):
                near = read(2 * k + t)
                far = roll4(read(layers - 1 - 2 * k - t))
                downs.append(jnp.where(upper, far, near))
                ups.append(jnp.where(upper, near, far))
            halo_out[base, item, k] = jnp.concatenate(downs, 0).astype(BF16)
            halo_out[base + 1, item, k] = jnp.concatenate(ups, 0).astype(BF16)
            return carry

        lax.fori_loop(start, stop or half // 2, step, 0, unroll=2)

    def unpack_halo(it, item, write, start=0, stop=None):
        base = 2 * it

        def step(k, carry):
            down = halo_in[base, item, k].astype(F32)
            up = halo_in[base + 1, item, k].astype(F32)
            for t in range(2):
                d, u = down[8 * t : 8 * t + 8], up[8 * t : 8 * t + 8]
                write(2 * k + t, jnp.where(upper, u, d))
                write(layers - 1 - 2 * k - t, roll4(jnp.where(upper, d, u)))
            return carry

        lax.fori_loop(start, stop or half // 2, step, 0, unroll=2)

    def unpack_fields(it, start, stop):
        for c in range(4):
            def write_field(l, v, c=c):
                beside[0, c, l] = v * beside_mask

            unpack_halo(it, c, write_field, start, stop)

    def z_sum(v):
        low = jnp.where(lane == 0, 0.0, pltpu.roll(v, 1, 1))
        high = jnp.where(lane == 127, 0.0, pltpu.roll(v, 127, 1))
        return low + high

    def relax(cur, across, layer, tiles, table):
        sums = [[None] * 4 for _ in range(2)]
        for c in range(4):
            a, b = cur[0][c], cur[1][c]
            a_up, b_up = pltpu.roll(a, 1, 0), pltpu.roll(b, 1, 0)
            a_dn, b_dn = pltpu.roll(a, 7, 0), pltpu.roll(b, 7, 0)
            for t in tiles:
                v = (a, b)[t]
                mine_up, mine_dn = ((a_up, a_dn), (b_up, b_dn))[t]
                other_up, other_dn = ((b_up, b_dn), (a_up, a_dn))[t]
                y_sum = jnp.where(row == 0, other_up, mine_up) + jnp.where(
                    row == 7, other_dn, mine_dn
                )
                sums[t][c] = across[t][c] + y_sum + z_sum(v)
        results = []
        for t in tiles:
            rr, ri = table[0, t, layer], table[1, t, layer]
            w = table[4, t, layer]
            fr = table[2, t, layer] + sums[t][0]
            fi = table[3, t, layer] + sums[t][1]
            ar = w * cur[t][0] + sums[t][2]
            ai = w * cur[t][1] + sums[t][3]
            results.append(
                (rr * fr - ri * fi, rr * fi + ri * fr, rr * ar + ri * ai, rr * ai - ri * ar)
            )
        return results

    buffers = (own, beside)

    def put(level, final, t, c, layer, value):
        if final and level == SWEEPS - 1:
            (forward, adjoint)[c // 2][c % 2, layer] = value
        else:
            buffers[t][(level + 1) % 2, c, layer] = value

    def sweep_run(level, first, count, tiles, final):
        src = level % 2

        def fetch(layer):
            return [[buffers[t][src, c, layer] for c in range(4)] for t in range(2)]

        values = [fetch(first + i) for i in range(-1, count + 1)]
        for i in range(count):
            low, cur, high = values[i], values[i + 1], values[i + 2]
            across = [[low[t][c] + high[t][c] for c in range(4)] for t in range(2)]
            results = relax(cur, across, first + i, tiles, coef)
            for t, result in zip(tiles, results):
                for c in range(4):
                    put(level, final, t, c, first + i, result[c])

    def sweep_inside(level, final):
        tiles = (0, 1) if level < SWEEPS - 1 else (0,)
        first, last = level + 1, layers - 2 - level
        total = last - first + 1
        trips = 2
        chunk = total // trips

        def step(k, carry):
            sweep_run(level, first + k * chunk, chunk, tiles, final)
            return carry

        lax.fori_loop(0, trips, step, 0)

    def sweep_end(level, ghosts, at_start, final):
        tiles = (0, 1) if level < SWEEPS - 1 else (0,)
        src = level % 2
        count = level + 1
        span = range(0, count) if at_start else range(layers - count, layers)

        def fetch(layer):
            if layer < 0 or layer >= layers:
                return ghosts
            return [[buffers[t][src, c, layer] for c in range(4)] for t in range(2)]

        values = {layer: fetch(layer) for layer in range(span[0] - 1, span[-1] + 2)}
        for layer in span:
            low, cur, high = values[layer - 1], values[layer], values[layer + 1]
            across = [[low[t][c] + high[t][c] for c in range(4)] for t in range(2)]
            results = relax(cur, across, layer, tiles, coef)
            for t, result in zip(tiles, results):
                for c in range(4):
                    put(level, final, t, c, layer, result[c])

    def next_sweep(level, span, ghosts):
        tiles = (0, 1) if level < SWEEPS - 1 else (0,)
        src, dst = level % 2, (level + 1) % 2

        def fetch(layer):
            if layer < 0:
                return ghosts
            return [[nxt[src, t, c, layer] for c in range(4)] for t in range(2)]

        values = {layer: fetch(layer) for layer in range(span[0] - 1, span[-1] + 2)}
        for layer in span:
            low, cur, high = values[layer - 1], values[layer], values[layer + 1]
            across = [[low[t][c] + high[t][c] for c in range(4)] for t in range(2)]
            for t, result in zip(tiles, relax(cur, across, layer, tiles, nxt_coef)):
                for c in range(4):
                    nxt[dst, t, c, layer] = result[c]

    def coefficients_of(tile, mask=None, read=None):
        def step(layer, carry):
            lab = read(layer)
            rr, ri = look(real_table, lab), look(imag_table, lab)
            if mask is not None:
                rr, ri = rr * mask, ri * mask
            coef[0, tile, layer] = rr
            coef[1, tile, layer] = ri
            coef[4, tile, layer] = look(weight_table, lab)
            return carry

        lax.fori_loop(0, layers, step, 0, unroll=4)

    pl.semaphore_wait(barrier, len(greeted))
    trace_copy().start()
    next_copies()[0].start()
    for load in loads[1:4]:
        load.wait()
    loads[4].start()
    pack_halo(0, 4, lambda l: coef[2, 0, l])
    pack_halo(0, 5, lambda l: coef[3, 0, l])
    pack_halo(0, 6, lambda l: labels[l].astype(F32))
    for copy in halo_copies(0, True):
        copy.start()
    for c in range(4):
        pack_halo(0, c, lambda l, c=c: own[0, c, l])
    for load in small_loads:
        load.wait()

    wave = jnp.zeros((8, 128), F32)
    absorb = jnp.zeros((8, 128), F32)
    weight_table = jnp.zeros((8, 128), F32)
    for m in range(16):
        wave = jnp.where(lane == m, wave_s[m], wave)
        absorb = jnp.where(lane == m, absorb_s[m], absorb)
        weight_table = jnp.where(lane == m, design_s[m], weight_table)
    shifted = 6.0 - wave
    modulus = shifted * shifted + absorb * absorb
    real_table = shifted / modulus
    imag_table = absorb / modulus

    def look(table, index):
        return jnp.take_along_axis(table, index, axis=1, mode="promise_in_bounds")

    position = row * 128 + lane

    def place(step, carry):
        for t in range(16):
            point = step * 16 + t
            carry = jnp.where(position == pairs_s[0, point], point, carry)
        return carry

    loads[0].wait()
    pairs = pairs_v[...]

    def gather_points(read_row, index):
        index_row = lax.shift_right_logical(index, 7)
        index_lane = lax.bitwise_and(index, 127)
        out = jnp.zeros((8, 128), F32)
        for r in range(8):
            source_row = jnp.broadcast_to(read_row(r), (8, 128))
            out = jnp.where(index_row == r, look(source_row, index_lane), out)
        return out

    def left_ghosts(it):
        return [[left_in[it, t, c] * not_first for c in range(4)] for t in range(2)]

    for it in range(ITERS):
        outgoing[it, 0] = jnp.zeros((32, 128), BF16)
        outgoing[it, n_sub + 1] = jnp.zeros((32, 128), BF16)

    for it in range(ITERS):
        if it == 0:
            trace_copy().wait_recv()
        facing = []
        for c in range(4):
            taken = gather_points(
                lambda r: (facing_in[c] if it == 0 else nxt[0, 0, c, 0])[r : r + 1, :], pairs
            )
            taken = taken * not_last
            facing.append(taken)
            face[1, c] = taken
            rows32[0, pl.ds(c, 8, stride=4), :] = taken - own[0, c, layers - 1]
        jumps[it, 0] = rows32[0].astype(BF16)
        for slot in order:
            jump_copy(it, slot).start()
        for t in range(2):
            last = [own[0, 2 * t + k, layers - 1] for k in range(2)]
            side_out[it, 16 * t : 16 * t + 16] = jnp.concatenate(last, 0).astype(BF16)
            side_out[it, 32 + 16 * t : 48 + 16 * t] = jnp.concatenate(
                facing[2 * t : 2 * t + 2], 0
            ).astype(BF16)
        for copy in side_copies(it):
            copy.start()

        if it == 0:
            for copy in halo_copies(0):
                copy.start()
            coefficients_of(0, read=lambda l: labels[l])
            next_copies()[1].start()
            inverse = lax.fori_loop(0, 64, place, jnp.zeros((8, 128), jnp.int32))
            inv_out[...] = inverse
            for copy in inverse_copies():
                copy.start()
            loads[4].wait()
        else:
            ghost_copy(0).wait_recv()
            for level in range(SWEEPS):
                sweep_end(level, left_ghosts(0), True, False)
            for c in range(4):
                pack_halo(it, c, lambda l, c=c: own[0, c, l], 0, 2)
            for copy in halo_copies(it, True):
                copy.start()
            for copy in halo_copies(it):
                copy.wait_recv()
            unpack_fields(it, 2, half // 2)
        contract = (((1,), (1,)), ((), ()))
        width = block.shape[1] // 2

        def product(columns):
            return lax.dot_general(
                stacked[0], block[0, columns], contract, preferred_element_type=F32
            ) + lax.dot_general(
                stacked[1], block[1, columns], contract, preferred_element_type=F32
            )

        for slot in order:
            jump_copy(it, slot).wait_recv()
        for i in range(0, n_sub, 4):
            first = [jumps[it, i + t].astype(F32) for t in range(4)]
            for r in range(8):
                k, odd = r // 2, r % 2
                plain, turned = [], []
                for t in (0, 2):
                    a = first[t][8 * k : 8 * k + 8]
                    b = first[t + 1][8 * k : 8 * k + 8]
                    v = jnp.where(upper, roll4(a) if odd else a, b if odd else roll4(b))
                    plain.append(v)
                    turned.append(jnp.where(even, -pltpu.roll(v, 7, 0), pltpu.roll(v, 1, 0)))
                columns = pl.ds(r * 128, 128)
                rows = pl.ds(4 * i, 16)
                stacked[0, rows, columns] = jnp.concatenate(plain, 0).astype(BF16)
                stacked[1, rows, columns] = jnp.concatenate(turned, 0).astype(BF16)
        for part in range(2):
            total = product(pl.ds(width * part, width))
            here = slice(16 * part, 16 * part + 16)
            for i in range(0, n_sub, 2):
                rows = total[4 * i : 4 * i + 8]
                evens, odds = [], []
                for k in range(2):
                    a = rows[:, 256 * k : 256 * k + 128]
                    b = rows[:, 256 * k + 128 : 256 * k + 256]
                    evens.append(jnp.where(upper, a, roll4(b)))
                    odds.append(jnp.where(upper, roll4(a), b))
                outgoing[it, source_of(i) + 1, here] = jnp.concatenate(evens, 0).astype(BF16)
                outgoing[it, source_of(i + 1) + 1, here] = jnp.concatenate(odds, 0).astype(BF16)
            for slot in order:
                product_copy(it, slot, part).start()
        for k in range(3):
            products[it, 0, k] = outgoing[it, me_s + k]

        if it == 0:
            for copy in halo_copies(it, True) + halo_copies(it):
                copy.wait_recv()
            unpack_fields(it, 0, half // 2)
            for c in range(2):
                def write_source(l, v, c=c):
                    coef[2 + c, 1, l] = v

                unpack_halo(0, 4 + c, write_source)

            def write_coef(l, v):
                lab = v.astype(jnp.int32)
                coef[0, 1, l] = look(real_table, lab) * beside_mask
                coef[1, 1, l] = look(imag_table, lab) * beside_mask
                coef[4, 1, l] = look(weight_table, lab)

            unpack_halo(0, 6, write_coef)
            for c in range(4):
                for layer in range(depth):
                    nxt_out[c, layer] = beside[0, c, layer]
            for copy in next_copies()[2:]:
                copy.start()
        else:
            for copy in halo_copies(it, True):
                copy.wait_recv()
            unpack_fields(it, 0, 2)
        final = it == ITERS - 1
        for level in range(SWEEPS):
            sweep_inside(level, final)
        if not final:
            for c in range(4):
                pack_halo(it + 1, c, lambda l, c=c: own[0, c, l], 2)
            for copy in halo_copies(it + 1):
                copy.start()

        if not final:
            for copy in next_copies():
                copy.wait_recv()
            next_sweep(0, range(1, depth - 1), None)
            next_sweep(1, range(2, depth - 2), None)
            for copy in inverse_copies():
                copy.wait_recv()
            inverse_beside = jnp.where(upper, inv_in[1], inv_in[0])
        for copy in side_copies(it):
            copy.wait_recv()
        for slot in order:
            product_copy(it, slot, 0).wait_recv()
            product_copy(it, slot, 1).wait_recv()
        for k in range(3):
            owner = owner_s[0, lax.rem(me_s + n_sub + k - 1, n_sub)]
            rows32[k] = products[it, slot_of(owner), k].astype(F32)
        right = [[], []]
        for c in range(4):
            moved = [rows32[k, pl.ds(c, 8, stride=4), :] for k in range(3)]
            pair = pl.ds(16 * (c // 2), 16)
            half_rows = slice(8 * (c % 2), 8 * (c % 2) + 8)
            lasts = [side_in[it, k, pair].astype(F32)[half_rows] for k in range(2)]
            pair = pl.ds(32 + 16 * (c // 2), 16)
            faces = [side_in[it, k, pair].astype(F32)[half_rows] for k in range(2)]
            right[0].append((face[1, c] + moved[1]) * not_last)
            right[1].append(
                jnp.where(upper, faces[1] + moved[2], faces[0] + moved[0]) * not_last
            )
            face[1, c] = own[0, c, layers - 1] - moved[1]
            face[0, c] = lasts[0] - moved[0]
            face[2, c] = lasts[1] - moved[2]
        left = [[], []]
        for c in range(4):
            left[0].append(gather_points(lambda r: face[1, c, r : r + 1, :], inverse))
            left[1].append(
                gather_points(
                    lambda r: jnp.where(
                        upper,
                        jnp.broadcast_to(face[2, c, r : r + 1, :], (8, 128)),
                        jnp.broadcast_to(face[0, c, r : r + 1, :], (8, 128)),
                    ),
                    inverse_beside,
                )
            )
            left_out[it, 0, c] = left[0][c]
            left_out[it, 1, c] = left[1][c]
        ghost_copy(it).start()
        if not final:
            for level in range(SWEEPS):
                next_sweep(level, ((0,), (0, 1), (0, 1), (0,))[level], left)
                sweep_end(level, right, False, final)
        else:
            trace_copy().wait_send()
            for copy in next_copies():
                copy.wait_send()
            for k in range(ITERS):
                for slot in order:
                    jump_copy(k, slot).wait_send()
                    product_copy(k, slot, 0).wait_send()
                    product_copy(k, slot, 1).wait_send()
                for copy in side_copies(k) + halo_copies(k) + halo_copies(k, True):
                    copy.wait_send()
            for copy in inverse_copies():
                copy.wait_send()
            ghost_copy(0).wait_send()
            ghost_copy(it).wait_recv()
            left = left_ghosts(it)
            for level in range(SWEEPS):
                sweep_end(level, left, True, final)
                sweep_end(level, right, False, final)
            ghost_copy(it).wait_send()


def store_kernel(forward_v, adjoint_v, forward_h, adjoint_h, sem):
    copies = [
        pltpu.make_async_copy(forward_v, forward_h, sem.at[0]),
        pltpu.make_async_copy(adjoint_v, adjoint_h, sem.at[1]),
    ]
    for copy in copies:
        copy.start()
    for copy in copies:
        copy.wait()


def solution(mesh):
    n_dom, n_sub = mesh.shape["dom"], mesh.shape["sub"]
    nx = 4 if n_sub % 4 == 0 and n_sub > 4 else 2

    def per_device(
        start_fields,
        source,
        labels,
        wavenumber2,
        absorption,
        design_weight,
        pairs,
        block_index,
        blocks,
    ):
        layers = labels.shape[0]
        points = pairs.shape[-1]
        slots = n_sub
        hbm = pl.BlockSpec(memory_space=pltpu.HBM)
        vmem = pl.BlockSpec(memory_space=pltpu.VMEM)
        out = jax.ShapeDtypeStruct((2,) + labels.shape, F32)
        dma = pltpu.SemaphoreType.DMA
        operands = [
            pltpu.with_memory_space_constraint(operand, pltpu.HBM)
            for operand in (
                pairs[0],
                block_index,
                wavenumber2,
                absorption,
                design_weight,
                pairs.reshape(8, 128),
                start_fields,
                source,
                labels,
                blocks,
            )
        ]
        results = pl.pallas_call(
            functools.partial(kernel, (n_dom, n_sub, nx)),
            out_shape=(out, out),
            in_specs=[hbm] * 10,
            out_specs=(vmem, vmem),
            scratch_shapes=[
                pltpu.SMEM((1, points), jnp.int32),
                pltpu.SMEM(block_index.shape, jnp.int32),
                pltpu.SMEM(wavenumber2.shape, F32),
                pltpu.SMEM(absorption.shape, F32),
                pltpu.SMEM(design_weight.shape, F32),
                pltpu.VMEM((8, 128), jnp.int32),
                pltpu.VMEM((2, 4, layers, 8, 128), F32),
                pltpu.VMEM((2, 4, layers, 8, 128), F32),
                pltpu.VMEM((5, 2, layers, 8, 128), F32),
                pltpu.VMEM((layers, 8, 128), jnp.int32),
                pltpu.VMEM((2, points, points), BF16),
                pltpu.VMEM((4, 8, 128), F32),
                pltpu.VMEM((ITERS, slots, 32, 128), BF16),
                pltpu.VMEM((2, 4 * slots, points), BF16),
                pltpu.VMEM((ITERS, slots + 2, 32, 128), BF16),
                pltpu.VMEM((ITERS, slots, 3, 32, 128), BF16),
                pltpu.VMEM((3, 32, 128), F32),
                pltpu.VMEM((3, 4, 8, 128), F32),
                pltpu.VMEM((ITERS, 2, 4, 8, 128), F32),
                pltpu.VMEM((ITERS, 2, 4, 8, 128), F32),
                pltpu.VMEM((ITERS, 64, 128), BF16),
                pltpu.VMEM((ITERS, 2, 64, 128), BF16),
                pltpu.VMEM((8, 128), jnp.int32),
                pltpu.VMEM((2, 8, 128), jnp.int32),
                pltpu.VMEM((4, 7, layers // 4, 16, 128), BF16),
                pltpu.VMEM((4, 7, layers // 4, 16, 128), BF16),
                dma((10,)),
                dma((2,)),
                dma((ITERS, slots)),
                dma((ITERS, slots)),
                dma((ITERS, slots, 2)),
                dma((ITERS, slots, 2)),
                dma((ITERS,)),
                dma((ITERS,)),
                dma((ITERS, 2)),
                dma((ITERS, 2)),
                dma((2,)),
                dma((2,)),
                dma((2 * ITERS, 2)),
                dma((2 * ITERS, 2)),
                pltpu.VMEM((2, 2, 4, SWEEPS + 1, 8, 128), F32),
                pltpu.VMEM((5, 2, SWEEPS, 8, 128), F32),
                pltpu.VMEM((4, SWEEPS + 1, 8, 128), F32),
                dma((4,)),
                dma((4,)),
            ],
            compiler_params=pltpu.CompilerParams(
                collective_id=0, has_side_effects=True, vmem_limit_bytes=20 * 1024 * 1024
            ),
        )(*operands)
        return pl.pallas_call(
            store_kernel,
            out_shape=(out, out),
            in_specs=[vmem, vmem],
            out_specs=(hbm, hbm),
            scratch_shapes=[dma((2,))],
            compiler_params=pltpu.CompilerParams(vmem_limit_bytes=4 * 1024 * 1024),
        )(*results)

    placed = (
        P(None, "dom", "sub", None),
        P(None, "dom", "sub", None),
        P("dom", "sub", None),
        P(),
        P(),
        P(),
        P("dom", "sub", None),
        P("dom", None),
        P("dom", "sub", None, None, None),
    )
    return jax.shard_map(
        per_device,
        mesh=mesh,
        in_specs=placed,
        out_specs=(P(None, "dom", "sub", None), P(None, "dom", "sub", None)),
        check_vma=False,
    )
```

```python
import functools

import jax
import jax.numpy as jnp
from jax import lax
from jax.experimental import pallas as pl
from jax.experimental.pallas import tpu as pltpu
from jax.sharding import PartitionSpec as P

SWEEPS = 4
ITERS = 2
MESH = pl.DeviceIdType.MESH
F32 = jnp.float32
BF16 = jnp.bfloat16


def torus_offsets(nx, ny):
    offsets = [(dx, dy) for dy in range(ny) for dx in range(nx)]
    hops = lambda o: min(o[0], nx - o[0]) + min(o[1], ny - o[1])
    order = sorted(range(1, nx * ny), key=lambda i: -hops(offsets[i]))
    return offsets, order


def kernel(
    shape,
    pairs_flat_h,
    owner_h,
    wave_h,
    absorb_h,
    design_h,
    pairs_h,
    fields_h,
    source_h,
    labels_h,
    blocks_h,
    forward,
    adjoint,
    pairs_s,
    owner_s,
    wave_s,
    absorb_s,
    design_s,
    pairs_v,
    own,
    beside,
    coef,
    labels,
    block,
    turned_block,
    facing_in,
    jumps,
    stacked,
    outgoing,
    products,
    rows32,
    face,
    left_out,
    left_in,
    side_out,
    side_in,
    inv_out,
    inv_in,
    halo_out,
    halo_in,
    load_sem,
    trace_sem,
    jump_send,
    jump_recv,
    prod_send,
    prod_recv,
    ghost_send,
    ghost_recv,
    side_send,
    side_recv,
    inv_send,
    inv_recv,
    halo_send,
    halo_recv,
    nxt,
    nxt_coef,
    nxt_out,
    nxt_send,
    nxt_recv,
):
    n_dom, n_sub, nx = shape
    ny = n_sub // nx
    layers = fields_h.shape[1]
    offsets, order = torus_offsets(nx, ny)
    me_d = lax.axis_index("dom")
    me_s = lax.axis_index("sub")
    my_x, my_y = lax.rem(me_s, nx), lax.div(me_s, nx)
    before_d, after_d = lax.rem(me_d + n_dom - 1, n_dom), lax.rem(me_d + 1, n_dom)
    before_s, after_s = lax.rem(me_s + n_sub - 1, n_sub), lax.rem(me_s + 1, n_sub)

    def member(slot):
        dx, dy = offsets[slot]
        return lax.rem(my_y + dy, ny) * nx + lax.rem(my_x + dx, nx)

    barrier = pltpu.get_barrier_semaphore()
    greeted = [(me_d, member(slot)) for slot in reversed(order)]
    greeted = [(before_d, me_s), (after_d, me_s)] + greeted
    for device in greeted:
        pl.semaphore_signal(barrier, inc=1, device_id=device, device_id_type=MESH)

    small_loads = [
        pltpu.make_async_copy(src, dst, load_sem.at[5 + k])
        for k, (src, dst) in enumerate(
            (
                (pairs_flat_h, pairs_s),
                (owner_h, owner_s),
                (wave_h, wave_s),
                (absorb_h, absorb_s),
                (design_h, design_s),
            )
        )
    ]
    for load in small_loads:
        load.start()
    loads = [
        pltpu.make_async_copy(pairs_h, pairs_v, load_sem.at[0]),
        pltpu.make_async_copy(fields_h, own.at[0], load_sem.at[1]),
        pltpu.make_async_copy(labels_h, labels, load_sem.at[2]),
        pltpu.make_async_copy(source_h, coef.at[2:4, 0], load_sem.at[3]),
        pltpu.make_async_copy(blocks_h.at[0, 0], block, load_sem.at[4]),
    ]
    for load in loads[:4]:
        load.start()

    row = lax.broadcasted_iota(jnp.int32, (8, 128), 0)
    lane = lax.broadcasted_iota(jnp.int32, (8, 128), 1)
    upper = row < 4
    even = lax.rem(row, 2) == 0
    not_first = jnp.where(me_d == 0, 0.0, 1.0).astype(F32)
    not_last = jnp.where(me_d == n_dom - 1, 0.0, 1.0).astype(F32)
    has_before = jnp.where(me_s == 0, 0.0, 1.0).astype(F32)
    has_after = jnp.where(me_s == n_sub - 1, 0.0, 1.0).astype(F32)
    beside_mask = jnp.where(upper, has_after, has_before)

    def roll4(value):
        return pltpu.roll(value, 4, 0)

    depth = nxt.shape[3]

    def trace_copy():
        return pltpu.make_async_remote_copy(
            src_ref=fields_h.at[:, 0],
            dst_ref=facing_in,
            send_sem=trace_sem.at[0],
            recv_sem=trace_sem.at[1],
            device_id=(before_d, me_s),
            device_id_type=MESH,
        )

    def next_copies():
        copies = []
        for k, (src, dst) in enumerate(
            (
                (fields_h.at[:, 0:depth], nxt.at[0, 0]),
                (coef.at[:, 0, 0 : depth - 1], nxt_coef.at[:, 0]),
                (nxt_out, nxt.at[0, 1]),
                (coef.at[:, 1, 0 : depth - 1], nxt_coef.at[:, 1]),
            )
        ):
            copies.append(
                pltpu.make_async_remote_copy(
                    src_ref=src,
                    dst_ref=dst,
                    send_sem=nxt_send.at[k],
                    recv_sem=nxt_recv.at[k],
                    device_id=(before_d, me_s),
                    device_id_type=MESH,
                )
            )
        return copies

    def source_of(slot):
        dx, dy = offsets[slot]
        return lax.rem(my_y + ny - dy, ny) * nx + lax.rem(my_x + nx - dx, nx)

    def slot_of(member_index):
        dx = lax.rem(lax.rem(member_index, nx) - my_x + nx, nx)
        dy = lax.rem(lax.div(member_index, nx) - my_y + ny, ny)
        return dy * nx + dx

    def jump_copy(it, slot):
        return pltpu.make_async_remote_copy(
            src_ref=jumps.at[it, 0],
            dst_ref=jumps.at[it, slot],
            send_sem=jump_send.at[it],
            recv_sem=jump_recv.at[it],
            device_id=(me_d, member(slot)),
            device_id_type=MESH,
        )

    def product_copy(it, slot):
        back = source_of(slot)
        return pltpu.make_async_remote_copy(
            src_ref=outgoing.at[it, pl.ds(back, 3)],
            dst_ref=products.at[it, slot],
            send_sem=prod_send.at[it],
            recv_sem=prod_recv.at[it],
            device_id=(me_d, back),
            device_id_type=MESH,
        )

    def all_of(ref, send_sem, recv_sem):
        return pltpu.make_async_remote_copy(
            src_ref=ref,
            dst_ref=ref,
            send_sem=send_sem,
            recv_sem=recv_sem,
            device_id=(me_d, after_s),
            device_id_type=MESH,
        )

    others = pl.ds(1, n_sub - 1)

    def all_jumps(it):
        return all_of(jumps.at[it, others], jump_send.at[it], jump_recv.at[it])

    def all_products(it):
        return all_of(products.at[it, others], prod_send.at[it], prod_recv.at[it])

    def all_sides(it):
        return all_of(side_in.at[it], side_send.at[it], side_recv.at[it])

    def all_inverses():
        return all_of(inv_in, inv_send, inv_recv)

    def ghost_copy(it):
        return pltpu.make_async_remote_copy(
            src_ref=left_out.at[it],
            dst_ref=left_in.at[it],
            send_sem=ghost_send.at[it],
            recv_sem=ghost_recv.at[it],
            device_id=(after_d, me_s),
            device_id_type=MESH,
        )

    def beside_copies(src, dst, send_sem, recv_sem):
        return [
            pltpu.make_async_remote_copy(
                src_ref=src,
                dst_ref=dst.at[k],
                send_sem=send_sem,
                recv_sem=recv_sem,
                device_id=(me_d, sub),
                device_id_type=MESH,
            )
            for k, sub in enumerate((after_s, before_s))
        ]

    def side_copies(it):
        return beside_copies(side_out.at[it], side_in.at[it], side_send.at[it], side_recv.at[it])

    def inverse_copies():
        return beside_copies(inv_out, inv_in, inv_send, inv_recv)

    def halo_part(it, second):
        groups = halo_out.shape[2]
        if it == 0:
            return (pl.ds(4, 3) if second else pl.ds(0, 4)), pl.ds(0, groups)
        return pl.ds(0, 4), (pl.ds(0, 2) if second else pl.ds(2, groups - 2))

    def halo_copies(it, second=False):
        copies = []
        for k, sub in enumerate((after_s, before_s)):
            part = (2 * it + k,) + halo_part(it, second)
            copies.append(
                pltpu.make_async_remote_copy(
                    src_ref=halo_out.at[part],
                    dst_ref=halo_in.at[part],
                    send_sem=halo_send.at[2 * it + second],
                    recv_sem=halo_recv.at[2 * it + second],
                    device_id=(me_d, sub),
                    device_id_type=MESH,
                )
            )
        return copies

    def all_halos(it, second=False):
        part = (pl.ds(2 * it, 2),) + halo_part(it, second)
        return all_of(halo_in.at[part], halo_send.at[2 * it + second], halo_recv.at[2 * it + second])

    half = layers // 2

    def pack_halo(it, item, read, start=0, stop=None):
        base = 2 * it

        def step(k, carry):
            downs, ups = [], []
            for t in range(2):
                near = read(2 * k + t)
                far = roll4(read(layers - 1 - 2 * k - t))
                downs.append(jnp.where(upper, far, near))
                ups.append(jnp.where(upper, near, far))
            halo_out[base, item, k] = jnp.concatenate(downs, 0).astype(BF16)
            halo_out[base + 1, item, k] = jnp.concatenate(ups, 0).astype(BF16)
            return carry

        lax.fori_loop(start, stop or half // 2, step, 0, unroll=2)

    def unpack_halo(it, item, write, start=0, stop=None):
        base = 2 * it

        def step(k, carry):
            down = halo_in[base, item, k].astype(F32)
            up = halo_in[base + 1, item, k].astype(F32)
            for t in range(2):
                d, u = down[8 * t : 8 * t + 8], up[8 * t : 8 * t + 8]
                write(2 * k + t, jnp.where(upper, u, d))
                write(layers - 1 - 2 * k - t, roll4(jnp.where(upper, d, u)))
            return carry

        lax.fori_loop(start, stop or half // 2, step, 0, unroll=2)

    def unpack_fields(it, start, stop):
        for c in range(4):
            def write_field(l, v, c=c):
                beside[0, c, l] = v * beside_mask

            unpack_halo(it, c, write_field, start, stop)

    def z_sum(v):
        low = jnp.where(lane == 0, 0.0, pltpu.roll(v, 1, 1))
        high = jnp.where(lane == 127, 0.0, pltpu.roll(v, 127, 1))
        return low + high

    def relax(cur, across, layer, tiles, table):
        sums = [[None] * 4 for _ in range(2)]
        for c in range(4):
            a, b = cur[0][c], cur[1][c]
            a_up, b_up = pltpu.roll(a, 1, 0), pltpu.roll(b, 1, 0)
            a_dn, b_dn = pltpu.roll(a, 7, 0), pltpu.roll(b, 7, 0)
            for t in tiles:
                v = (a, b)[t]
                mine_up, mine_dn = ((a_up, a_dn), (b_up, b_dn))[t]
                other_up, other_dn = ((b_up, b_dn), (a_up, a_dn))[t]
                y_sum = jnp.where(row == 0, other_up, mine_up) + jnp.where(
                    row == 7, other_dn, mine_dn
                )
                sums[t][c] = across[t][c] + y_sum + z_sum(v)
        results = []
        for t in tiles:
            rr, ri = table[0, t, layer], table[1, t, layer]
            w = table[4, t, layer]
            fr = table[2, t, layer] + sums[t][0]
            fi = table[3, t, layer] + sums[t][1]
            ar = w * cur[t][0] + sums[t][2]
            ai = w * cur[t][1] + sums[t][3]
            results.append(
                (rr * fr - ri * fi, rr * fi + ri * fr, rr * ar + ri * ai, rr * ai - ri * ar)
            )
        return results

    buffers = (own, beside)

    def put(level, final, t, c, layer, value):
        if final and level == SWEEPS - 1:
            (forward, adjoint)[c // 2][c % 2, layer] = value
        else:
            buffers[t][(level + 1) % 2, c, layer] = value

    def sweep_run(level, first, count, tiles, final):
        src = level % 2

        def fetch(layer):
            return [[buffers[t][src, c, layer] for c in range(4)] for t in range(2)]

        values = [fetch(first + i) for i in range(-1, count + 1)]
        for i in range(count):
            low, cur, high = values[i], values[i + 1], values[i + 2]
            across = [[low[t][c] + high[t][c] for c in range(4)] for t in range(2)]
            results = relax(cur, across, first + i, tiles, coef)
            for t, result in zip(tiles, results):
                for c in range(4):
                    put(level, final, t, c, first + i, result[c])

    def sweep_inside(level, final):
        tiles = (0, 1) if level < SWEEPS - 1 else (0,)
        first, last = level + 1, layers - 2 - level
        total = last - first + 1
        trips = 2
        chunk = total // trips

        def step(k, carry):
            sweep_run(level, first + k * chunk, chunk, tiles, final)
            return carry

        lax.fori_loop(0, trips, step, 0)

    def sweep_end(level, ghosts, at_start, final):
        tiles = (0, 1) if level < SWEEPS - 1 else (0,)
        src = level % 2
        count = level + 1
        span = range(0, count) if at_start else range(layers - count, layers)

        def fetch(layer):
            if layer < 0 or layer >= layers:
                return ghosts
            return [[buffers[t][src, c, layer] for c in range(4)] for t in range(2)]

        values = {layer: fetch(layer) for layer in range(span[0] - 1, span[-1] + 2)}
        for layer in span:
            low, cur, high = values[layer - 1], values[layer], values[layer + 1]
            across = [[low[t][c] + high[t][c] for c in range(4)] for t in range(2)]
            results = relax(cur, across, layer, tiles, coef)
            for t, result in zip(tiles, results):
                for c in range(4):
                    put(level, final, t, c, layer, result[c])

    def next_sweep(level, span, ghosts):
        tiles = (0, 1) if level < SWEEPS - 1 else (0,)
        src, dst = level % 2, (level + 1) % 2

        def fetch(layer):
            if layer < 0:
                return ghosts
            return [[nxt[src, t, c, layer] for c in range(4)] for t in range(2)]

        values = {layer: fetch(layer) for layer in range(span[0] - 1, span[-1] + 2)}
        for layer in span:
            low, cur, high = values[layer - 1], values[layer], values[layer + 1]
            across = [[low[t][c] + high[t][c] for c in range(4)] for t in range(2)]
            for t, result in zip(tiles, relax(cur, across, layer, tiles, nxt_coef)):
                for c in range(4):
                    nxt[dst, t, c, layer] = result[c]

    def coefficients_of(tile, mask=None, read=None):
        def step(layer, carry):
            lab = read(layer)
            rr, ri = look(real_table, lab), look(imag_table, lab)
            if mask is not None:
                rr, ri = rr * mask, ri * mask
            coef[0, tile, layer] = rr
            coef[1, tile, layer] = ri
            coef[4, tile, layer] = look(weight_table, lab)
            return carry

        lax.fori_loop(0, layers, step, 0, unroll=4)

    pl.semaphore_wait(barrier, len(greeted))
    trace_copy().start()
    next_copies()[0].start()
    for load in loads[1:4]:
        load.wait()
    loads[4].start()
    pack_halo(0, 4, lambda l: coef[2, 0, l])
    pack_halo(0, 5, lambda l: coef[3, 0, l])
    pack_halo(0, 6, lambda l: labels[l].astype(F32))
    for copy in halo_copies(0, True):
        copy.start()
    for c in range(4):
        pack_halo(0, c, lambda l, c=c: own[0, c, l])
    for load in small_loads:
        load.wait()

    wave = jnp.zeros((8, 128), F32)
    absorb = jnp.zeros((8, 128), F32)
    weight_table = jnp.zeros((8, 128), F32)
    for m in range(16):
        wave = jnp.where(lane == m, wave_s[m], wave)
        absorb = jnp.where(lane == m, absorb_s[m], absorb)
        weight_table = jnp.where(lane == m, design_s[m], weight_table)
    shifted = 6.0 - wave
    modulus = shifted * shifted + absorb * absorb
    real_table = shifted / modulus
    imag_table = absorb / modulus

    def look(table, index):
        return jnp.take_along_axis(table, index, axis=1, mode="promise_in_bounds")

    position = row * 128 + lane

    def place(step, carry):
        for t in range(16):
            point = step * 16 + t
            carry = jnp.where(position == pairs_s[0, point], point, carry)
        return carry

    loads[0].wait()
    pairs = pairs_v[...]

    def gather_points(read_row, index):
        index_row = lax.shift_right_logical(index, 7)
        index_lane = lax.bitwise_and(index, 127)
        out = jnp.zeros((8, 128), F32)
        for r in range(8):
            source_row = jnp.broadcast_to(read_row(r), (8, 128))
            out = jnp.where(index_row == r, look(source_row, index_lane), out)
        return out

    def left_ghosts(it):
        return [[left_in[it, t, c] * not_first for c in range(4)] for t in range(2)]

    for it in range(ITERS):
        outgoing[it, 0] = jnp.zeros((32, 128), BF16)
        outgoing[it, n_sub + 1] = jnp.zeros((32, 128), BF16)

    for it in range(ITERS):
        if it == 0:
            trace_copy().wait_recv()
        facing = []
        for c in range(4):
            taken = gather_points(
                lambda r: (facing_in[c] if it == 0 else nxt[0, 0, c, 0])[r : r + 1, :], pairs
            )
            taken = taken * not_last
            facing.append(taken)
            face[1, c] = taken
            rows32[0, pl.ds(c, 8, stride=4), :] = taken - own[0, c, layers - 1]
        jumps[it, 0] = rows32[0].astype(BF16)
        for slot in order:
            jump_copy(it, slot).start()
        for t in range(2):
            last = [own[0, 2 * t + k, layers - 1] for k in range(2)]
            side_out[it, 16 * t : 16 * t + 16] = jnp.concatenate(last, 0).astype(BF16)
            side_out[it, 32 + 16 * t : 48 + 16 * t] = jnp.concatenate(
                facing[2 * t : 2 * t + 2], 0
            ).astype(BF16)
        for copy in side_copies(it):
            copy.start()

        if it == 0:
            for copy in halo_copies(0):
                copy.start()
            coefficients_of(0, read=lambda l: labels[l])
            next_copies()[1].start()
            inverse = lax.fori_loop(0, 64, place, jnp.zeros((8, 128), jnp.int32))
            inv_out[...] = inverse
            for copy in inverse_copies():
                copy.start()
            loads[4].wait()

            def turn(k, carry):
                rows = pl.ds(pl.multiple_of(128 * k, 128), 128)
                for h in range(2):
                    turned_block[h, :, rows] = jnp.transpose(block[h, rows, :])
                return carry

            lax.fori_loop(0, block.shape[1] // 128, turn, 0)
        else:
            ghost_copy(0).wait_recv()
            for level in range(SWEEPS):
                sweep_end(level, left_ghosts(0), True, False)
            for c in range(4):
                pack_halo(it, c, lambda l, c=c: own[0, c, l], 0, 2)
            for copy in halo_copies(it, True):
                copy.start()
            all_halos(it).wait_recv()
            unpack_fields(it, 2, half // 2)
        contract = (((1,), (0,)), ((), ()))
        width = block.shape[1] // 2

        def product(columns):
            return lax.dot_general(
                stacked[0], turned_block[0, :, columns], contract, preferred_element_type=F32
            ) + lax.dot_general(
                stacked[1], turned_block[1, :, columns], contract, preferred_element_type=F32
            )

        all_jumps(it).wait_recv()
        for i in range(0, n_sub, 4):
            first = [jumps[it, i + t].astype(F32) for t in range(4)]
            for r in range(8):
                k, odd = r // 2, r % 2
                plain, turned = [], []
                for t in (0, 2):
                    a = first[t][8 * k : 8 * k + 8]
                    b = first[t + 1][8 * k : 8 * k + 8]
                    v = jnp.where(upper, roll4(a) if odd else a, b if odd else roll4(b))
                    plain.append(v)
                    turned.append(jnp.where(even, -pltpu.roll(v, 7, 0), pltpu.roll(v, 1, 0)))
                columns = pl.ds(r * 128, 128)
                rows = pl.ds(4 * i, 16)
                stacked[0, rows, columns] = jnp.concatenate(plain, 0).astype(BF16)
                stacked[1, rows, columns] = jnp.concatenate(turned, 0).astype(BF16)
        for part in range(2):
            total = product(pl.ds(width * part, width))
            here = slice(16 * part, 16 * part + 16)
            for i in range(0, n_sub, 2):
                rows = total[4 * i : 4 * i + 8]
                evens, odds = [], []
                for k in range(2):
                    a = rows[:, 256 * k : 256 * k + 128]
                    b = rows[:, 256 * k + 128 : 256 * k + 256]
                    evens.append(jnp.where(upper, a, roll4(b)))
                    odds.append(jnp.where(upper, roll4(a), b))
                outgoing[it, source_of(i) + 1, here] = jnp.concatenate(evens, 0).astype(BF16)
                outgoing[it, source_of(i + 1) + 1, here] = jnp.concatenate(odds, 0).astype(BF16)
        for slot in order:
            product_copy(it, slot).start()
        for k in range(3):
            products[it, 0, k] = outgoing[it, me_s + k]

        if it == 0:
            all_halos(it, True).wait_recv()
            all_halos(it).wait_recv()
            unpack_fields(it, 0, half // 2)
            for c in range(2):
                def write_source(l, v, c=c):
                    coef[2 + c, 1, l] = v

                unpack_halo(0, 4 + c, write_source)

            def write_coef(l, v):
                lab = v.astype(jnp.int32)
                coef[0, 1, l] = look(real_table, lab) * beside_mask
                coef[1, 1, l] = look(imag_table, lab) * beside_mask
                coef[4, 1, l] = look(weight_table, lab)

            unpack_halo(0, 6, write_coef)
            for c in range(4):
                for layer in range(depth):
                    nxt_out[c, layer] = beside[0, c, layer]
            for copy in next_copies()[2:]:
                copy.start()
        else:
            all_halos(it, True).wait_recv()
            unpack_fields(it, 0, 2)
        final = it == ITERS - 1
        for level in range(SWEEPS):
            sweep_inside(level, final)
        if not final:
            for c in range(4):
                pack_halo(it + 1, c, lambda l, c=c: own[0, c, l], 2)
            for copy in halo_copies(it + 1):
                copy.start()

        if not final:
            for copy in next_copies():
                copy.wait_recv()
            next_sweep(0, range(1, depth - 1), None)
            next_sweep(1, range(2, depth - 2), None)
            all_inverses().wait_recv()
            inverse_beside = jnp.where(upper, inv_in[1], inv_in[0])
        all_sides(it).wait_recv()
        all_products(it).wait_recv()
        for k in range(3):
            owner = owner_s[0, lax.rem(me_s + n_sub + k - 1, n_sub)]
            rows32[k] = products[it, slot_of(owner), k].astype(F32)
        right = [[], []]
        for c in range(4):
            moved = [rows32[k, pl.ds(c, 8, stride=4), :] for k in range(3)]
            pair = pl.ds(16 * (c // 2), 16)
            half_rows = slice(8 * (c % 2), 8 * (c % 2) + 8)
            lasts = [side_in[it, k, pair].astype(F32)[half_rows] for k in range(2)]
            pair = pl.ds(32 + 16 * (c // 2), 16)
            faces = [side_in[it, k, pair].astype(F32)[half_rows] for k in range(2)]
            right[0].append((face[1, c] + moved[1]) * not_last)
            right[1].append(
                jnp.where(upper, faces[1] + moved[2], faces[0] + moved[0]) * not_last
            )
            face[1, c] = own[0, c, layers - 1] - moved[1]
            face[0, c] = lasts[0] - moved[0]
            face[2, c] = lasts[1] - moved[2]
        left = [[], []]
        for c in range(4):
            left[0].append(gather_points(lambda r: face[1, c, r : r + 1, :], inverse))
            left[1].append(
                gather_points(
                    lambda r: jnp.where(
                        upper,
                        jnp.broadcast_to(face[2, c, r : r + 1, :], (8, 128)),
                        jnp.broadcast_to(face[0, c, r : r + 1, :], (8, 128)),
                    ),
                    inverse_beside,
                )
            )
            left_out[it, 0, c] = left[0][c]
            left_out[it, 1, c] = left[1][c]
        ghost_copy(it).start()
        if not final:
            for level in range(SWEEPS):
                next_sweep(level, ((0,), (0, 1), (0, 1), (0,))[level], left)
                sweep_end(level, right, False, final)
        else:
            trace_copy().wait_send()
            for copy in next_copies():
                copy.wait_send()
            for k in range(ITERS):
                for copy in (
                    all_jumps(k),
                    all_products(k),
                    all_sides(k),
                    all_halos(k),
                    all_halos(k, True),
                ):
                    copy.wait_send()
            all_inverses().wait_send()
            ghost_copy(0).wait_send()
            ghost_copy(it).wait_recv()
            left = left_ghosts(it)
            for level in range(SWEEPS):
                sweep_end(level, left, True, final)
                sweep_end(level, right, False, final)
            ghost_copy(it).wait_send()


def store_kernel(forward_v, adjoint_v, forward_h, adjoint_h, sem):
    copies = [
        pltpu.make_async_copy(forward_v, forward_h, sem.at[0]),
        pltpu.make_async_copy(adjoint_v, adjoint_h, sem.at[1]),
    ]
    for copy in copies:
        copy.start()
    for copy in copies:
        copy.wait()


def solution(mesh):
    n_dom, n_sub = mesh.shape["dom"], mesh.shape["sub"]
    nx = 4 if n_sub % 4 == 0 and n_sub > 4 else 2

    def per_device(
        start_fields,
        source,
        labels,
        wavenumber2,
        absorption,
        design_weight,
        pairs,
        block_index,
        blocks,
    ):
        layers = labels.shape[0]
        points = pairs.shape[-1]
        slots = n_sub
        hbm = pl.BlockSpec(memory_space=pltpu.HBM)
        vmem = pl.BlockSpec(memory_space=pltpu.VMEM)
        out = jax.ShapeDtypeStruct((2,) + labels.shape, F32)
        dma = pltpu.SemaphoreType.DMA
        operands = [
            pltpu.with_memory_space_constraint(operand, pltpu.HBM)
            for operand in (
                pairs[0],
                block_index,
                wavenumber2,
                absorption,
                design_weight,
                pairs.reshape(8, 128),
                start_fields,
                source,
                labels,
                blocks,
            )
        ]
        results = pl.pallas_call(
            functools.partial(kernel, (n_dom, n_sub, nx)),
            out_shape=(out, out),
            in_specs=[hbm] * 10,
            out_specs=(vmem, vmem),
            scratch_shapes=[
                pltpu.SMEM((1, points), jnp.int32),
                pltpu.SMEM(block_index.shape, jnp.int32),
                pltpu.SMEM(wavenumber2.shape, F32),
                pltpu.SMEM(absorption.shape, F32),
                pltpu.SMEM(design_weight.shape, F32),
                pltpu.VMEM((8, 128), jnp.int32),
                pltpu.VMEM((2, 4, layers, 8, 128), F32),
                pltpu.VMEM((2, 4, layers, 8, 128), F32),
                pltpu.VMEM((5, 2, layers, 8, 128), F32),
                pltpu.VMEM((layers, 8, 128), jnp.int32),
                pltpu.VMEM((2, points, points), BF16),
                pltpu.VMEM((2, points, points), BF16),
                pltpu.VMEM((4, 8, 128), F32),
                pltpu.VMEM((ITERS, slots, 32, 128), BF16),
                pltpu.VMEM((2, 4 * slots, points), BF16),
                pltpu.VMEM((ITERS, slots + 2, 32, 128), BF16),
                pltpu.VMEM((ITERS, slots, 3, 32, 128), BF16),
                pltpu.VMEM((3, 32, 128), F32),
                pltpu.VMEM((3, 4, 8, 128), F32),
                pltpu.VMEM((ITERS, 2, 4, 8, 128), F32),
                pltpu.VMEM((ITERS, 2, 4, 8, 128), F32),
                pltpu.VMEM((ITERS, 64, 128), BF16),
                pltpu.VMEM((ITERS, 2, 64, 128), BF16),
                pltpu.VMEM((8, 128), jnp.int32),
                pltpu.VMEM((2, 8, 128), jnp.int32),
                pltpu.VMEM((4, 7, layers // 4, 16, 128), BF16),
                pltpu.VMEM((4, 7, layers // 4, 16, 128), BF16),
                dma((10,)),
                dma((2,)),
                dma((ITERS,)),
                dma((ITERS,)),
                dma((ITERS,)),
                dma((ITERS,)),
                dma((ITERS,)),
                dma((ITERS,)),
                dma((ITERS,)),
                dma((ITERS,)),
                dma(()),
                dma(()),
                dma((2 * ITERS,)),
                dma((2 * ITERS,)),
                pltpu.VMEM((2, 2, 4, SWEEPS + 1, 8, 128), F32),
                pltpu.VMEM((5, 2, SWEEPS, 8, 128), F32),
                pltpu.VMEM((4, SWEEPS + 1, 8, 128), F32),
                dma((4,)),
                dma((4,)),
            ],
            compiler_params=pltpu.CompilerParams(
                collective_id=0, has_side_effects=True, vmem_limit_bytes=20 * 1024 * 1024
            ),
        )(*operands)
        return pl.pallas_call(
            store_kernel,
            out_shape=(out, out),
            in_specs=[vmem, vmem],
            out_specs=(hbm, hbm),
            scratch_shapes=[dma((2,))],
            compiler_params=pltpu.CompilerParams(vmem_limit_bytes=4 * 1024 * 1024),
        )(*results)

    placed = (
        P(None, "dom", "sub", None),
        P(None, "dom", "sub", None),
        P("dom", "sub", None),
        P(),
        P(),
        P(),
        P("dom", "sub", None),
        P("dom", None),
        P("dom", "sub", None, None, None),
    )
    return jax.shard_map(
        per_device,
        mesh=mesh,
        in_specs=placed,
        out_specs=(P(None, "dom", "sub", None), P(None, "dom", "sub", None)),
        check_vma=False,
    )
```

```python
import functools

import jax
import jax.numpy as jnp
from jax import lax
from jax.experimental import pallas as pl
from jax.experimental.pallas import tpu as pltpu
from jax.sharding import PartitionSpec as P

SWEEPS = 4
ITERS = 2
MESH = pl.DeviceIdType.MESH
F32 = jnp.float32
BF16 = jnp.bfloat16


def torus_offsets(nx, ny):
    offsets = [(dx, dy) for dy in range(ny) for dx in range(nx)]
    hops = lambda o: min(o[0], nx - o[0]) + min(o[1], ny - o[1])
    order = sorted(range(1, nx * ny), key=lambda i: -hops(offsets[i]))
    return offsets, order


def kernel(
    shape,
    pairs_flat_h,
    owner_h,
    wave_h,
    absorb_h,
    design_h,
    pairs_h,
    fields_h,
    source_h,
    labels_h,
    blocks_h,
    forward,
    adjoint,
    pairs_s,
    owner_s,
    wave_s,
    absorb_s,
    design_s,
    pairs_v,
    own,
    beside,
    coef,
    labels,
    block,
    turned_block,
    facing_in,
    jumps,
    stacked,
    outgoing,
    products,
    rows32,
    face,
    left_out,
    left_in,
    side_out,
    side_in,
    inv_out,
    inv_in,
    halo_out,
    halo_in,
    load_sem,
    trace_sem,
    jump_send,
    jump_recv,
    prod_send,
    prod_recv,
    ghost_send,
    ghost_recv,
    side_send,
    side_recv,
    inv_send,
    inv_recv,
    halo_send,
    halo_recv,
    nxt,
    nxt_coef,
    nxt_out,
    nxt_send,
    nxt_recv,
):
    n_dom, n_sub, nx = shape
    ny = n_sub // nx
    layers = fields_h.shape[1]
    offsets, order = torus_offsets(nx, ny)
    me_d = lax.axis_index("dom")
    me_s = lax.axis_index("sub")
    my_x, my_y = lax.rem(me_s, nx), lax.div(me_s, nx)
    before_d, after_d = lax.rem(me_d + n_dom - 1, n_dom), lax.rem(me_d + 1, n_dom)
    before_s, after_s = lax.rem(me_s + n_sub - 1, n_sub), lax.rem(me_s + 1, n_sub)

    def member(slot):
        dx, dy = offsets[slot]
        return lax.rem(my_y + dy, ny) * nx + lax.rem(my_x + dx, nx)

    barrier = pltpu.get_barrier_semaphore()
    greeted = [(me_d, member(slot)) for slot in reversed(order)]
    greeted = [(before_d, me_s), (after_d, me_s)] + greeted
    for device in greeted:
        pl.semaphore_signal(barrier, inc=1, device_id=device, device_id_type=MESH)

    small_loads = [
        pltpu.make_async_copy(src, dst, load_sem.at[5 + k])
        for k, (src, dst) in enumerate(
            (
                (pairs_flat_h, pairs_s),
                (owner_h, owner_s),
                (wave_h, wave_s),
                (absorb_h, absorb_s),
                (design_h, design_s),
            )
        )
    ]
    for load in small_loads:
        load.start()
    loads = [
        pltpu.make_async_copy(pairs_h, pairs_v, load_sem.at[0]),
        pltpu.make_async_copy(fields_h, own.at[0], load_sem.at[1]),
        pltpu.make_async_copy(labels_h, labels, load_sem.at[2]),
        pltpu.make_async_copy(source_h, coef.at[2:4, 0], load_sem.at[3]),
        pltpu.make_async_copy(blocks_h.at[0, 0], block, load_sem.at[4]),
    ]
    for load in loads[:4]:
        load.start()

    row = lax.broadcasted_iota(jnp.int32, (8, 128), 0)
    lane = lax.broadcasted_iota(jnp.int32, (8, 128), 1)
    upper = row < 4
    even = lax.rem(row, 2) == 0
    not_first = jnp.where(me_d == 0, 0.0, 1.0).astype(F32)
    not_last = jnp.where(me_d == n_dom - 1, 0.0, 1.0).astype(F32)
    has_before = jnp.where(me_s == 0, 0.0, 1.0).astype(F32)
    has_after = jnp.where(me_s == n_sub - 1, 0.0, 1.0).astype(F32)
    beside_mask = jnp.where(upper, has_after, has_before)

    def roll4(value):
        return pltpu.roll(value, 4, 0)

    depth = nxt.shape[3]

    def trace_copy():
        return pltpu.make_async_remote_copy(
            src_ref=own.at[0, :, 0],
            dst_ref=facing_in,
            send_sem=trace_sem.at[0],
            recv_sem=trace_sem.at[1],
            device_id=(before_d, me_s),
            device_id_type=MESH,
        )

    def next_copies():
        copies = []
        for k, (src, dst) in enumerate(
            (
                (fields_h.at[:, 0:depth], nxt.at[0, 0]),
                (coef.at[:, 0, 0 : depth - 1], nxt_coef.at[:, 0]),
                (nxt_out, nxt.at[0, 1]),
                (coef.at[:, 1, 0 : depth - 1], nxt_coef.at[:, 1]),
            )
        ):
            copies.append(
                pltpu.make_async_remote_copy(
                    src_ref=src,
                    dst_ref=dst,
                    send_sem=nxt_send.at[k],
                    recv_sem=nxt_recv.at[k],
                    device_id=(before_d, me_s),
                    device_id_type=MESH,
                )
            )
        return copies

    def source_of(slot):
        dx, dy = offsets[slot]
        return lax.rem(my_y + ny - dy, ny) * nx + lax.rem(my_x + nx - dx, nx)

    def slot_of(member_index):
        dx = lax.rem(lax.rem(member_index, nx) - my_x + nx, nx)
        dy = lax.rem(lax.div(member_index, nx) - my_y + ny, ny)
        return dy * nx + dx

    def jump_copy(it, slot):
        return pltpu.make_async_remote_copy(
            src_ref=jumps.at[it, 0],
            dst_ref=jumps.at[it, slot],
            send_sem=jump_send.at[it],
            recv_sem=jump_recv.at[it],
            device_id=(me_d, member(slot)),
            device_id_type=MESH,
        )

    def product_copy(it, slot):
        back = source_of(slot)
        return pltpu.make_async_remote_copy(
            src_ref=outgoing.at[it, pl.ds(back, 3)],
            dst_ref=products.at[it, slot],
            send_sem=prod_send.at[it],
            recv_sem=prod_recv.at[it],
            device_id=(me_d, back),
            device_id_type=MESH,
        )

    def all_of(ref, send_sem, recv_sem):
        return pltpu.make_async_remote_copy(
            src_ref=ref,
            dst_ref=ref,
            send_sem=send_sem,
            recv_sem=recv_sem,
            device_id=(me_d, after_s),
            device_id_type=MESH,
        )

    others = pl.ds(1, n_sub - 1)

    def all_jumps(it):
        return all_of(jumps.at[it, others], jump_send.at[it], jump_recv.at[it])

    def all_products(it):
        return all_of(products.at[it, others], prod_send.at[it], prod_recv.at[it])

    def all_sides(it):
        return all_of(side_in.at[it], side_send.at[it], side_recv.at[it])

    def all_inverses():
        return all_of(inv_in, inv_send, inv_recv)

    def ghost_copy(it):
        return pltpu.make_async_remote_copy(
            src_ref=left_out.at[it],
            dst_ref=left_in.at[it],
            send_sem=ghost_send.at[it],
            recv_sem=ghost_recv.at[it],
            device_id=(after_d, me_s),
            device_id_type=MESH,
        )

    def beside_copies(src, dst, send_sem, recv_sem):
        return [
            pltpu.make_async_remote_copy(
                src_ref=src,
                dst_ref=dst.at[k],
                send_sem=send_sem,
                recv_sem=recv_sem,
                device_id=(me_d, sub),
                device_id_type=MESH,
            )
            for k, sub in enumerate((after_s, before_s))
        ]

    def side_copies(it):
        return beside_copies(side_out.at[it], side_in.at[it], side_send.at[it], side_recv.at[it])

    def inverse_copies():
        return beside_copies(inv_out, inv_in, inv_send, inv_recv)

    def halo_part(it, second):
        groups = halo_out.shape[2]
        if it == 0:
            return (pl.ds(4, 3) if second else pl.ds(0, 4)), pl.ds(0, groups)
        return pl.ds(0, 4), (pl.ds(0, 2) if second else pl.ds(2, groups - 2))

    def halo_copies(it, second=False):
        copies = []
        for k, sub in enumerate((after_s, before_s)):
            part = (2 * it + k,) + halo_part(it, second)
            copies.append(
                pltpu.make_async_remote_copy(
                    src_ref=halo_out.at[part],
                    dst_ref=halo_in.at[part],
                    send_sem=halo_send.at[2 * it + second],
                    recv_sem=halo_recv.at[2 * it + second],
                    device_id=(me_d, sub),
                    device_id_type=MESH,
                )
            )
        return copies

    def all_halos(it, second=False):
        part = (pl.ds(2 * it, 2),) + halo_part(it, second)
        return all_of(halo_in.at[part], halo_send.at[2 * it + second], halo_recv.at[2 * it + second])

    half = layers // 2

    def pack_halo(it, item, read, start=0, stop=None):
        base = 2 * it

        def step(k, carry):
            downs, ups = [], []
            for t in range(2):
                near = read(2 * k + t)
                far = roll4(read(layers - 1 - 2 * k - t))
                downs.append(jnp.where(upper, far, near))
                ups.append(jnp.where(upper, near, far))
            halo_out[base, item, k] = jnp.concatenate(downs, 0).astype(BF16)
            halo_out[base + 1, item, k] = jnp.concatenate(ups, 0).astype(BF16)
            return carry

        lax.fori_loop(start, stop or half // 2, step, 0, unroll=2)

    def unpack_halo(it, item, write, start=0, stop=None):
        base = 2 * it

        def step(k, carry):
            down = halo_in[base, item, k].astype(F32)
            up = halo_in[base + 1, item, k].astype(F32)
            for t in range(2):
                d, u = down[8 * t : 8 * t + 8], up[8 * t : 8 * t + 8]
                write(2 * k + t, jnp.where(upper, u, d))
                write(layers - 1 - 2 * k - t, roll4(jnp.where(upper, d, u)))
            return carry

        lax.fori_loop(start, stop or half // 2, step, 0, unroll=2)

    def unpack_fields(it, start, stop):
        for c in range(4):
            def write_field(l, v, c=c):
                beside[0, c, l] = v * beside_mask

            unpack_halo(it, c, write_field, start, stop)

    def z_sum(v):
        low = jnp.where(lane == 0, 0.0, pltpu.roll(v, 1, 1))
        high = jnp.where(lane == 127, 0.0, pltpu.roll(v, 127, 1))
        return low + high

    def relax(cur, across, layer, tiles, table):
        sums = [[None] * 4 for _ in range(2)]
        for c in range(4):
            a, b = cur[0][c], cur[1][c]
            a_up, b_up = pltpu.roll(a, 1, 0), pltpu.roll(b, 1, 0)
            a_dn, b_dn = pltpu.roll(a, 7, 0), pltpu.roll(b, 7, 0)
            for t in tiles:
                v = (a, b)[t]
                mine_up, mine_dn = ((a_up, a_dn), (b_up, b_dn))[t]
                other_up, other_dn = ((b_up, b_dn), (a_up, a_dn))[t]
                y_sum = jnp.where(row == 0, other_up, mine_up) + jnp.where(
                    row == 7, other_dn, mine_dn
                )
                sums[t][c] = across[t][c] + y_sum + z_sum(v)
        results = []
        for t in tiles:
            rr, ri = table[0, t, layer], table[1, t, layer]
            w = table[4, t, layer]
            fr = table[2, t, layer] + sums[t][0]
            fi = table[3, t, layer] + sums[t][1]
            ar = w * cur[t][0] + sums[t][2]
            ai = w * cur[t][1] + sums[t][3]
            results.append(
                (rr * fr - ri * fi, rr * fi + ri * fr, rr * ar + ri * ai, rr * ai - ri * ar)
            )
        return results

    buffers = (own, beside)

    def put(level, final, t, c, layer, value):
        if final and level == SWEEPS - 1:
            (forward, adjoint)[c // 2][c % 2, layer] = value
        else:
            buffers[t][(level + 1) % 2, c, layer] = value

    def sweep_run(level, first, count, tiles, final):
        src = level % 2

        def fetch(layer):
            return [[buffers[t][src, c, layer] for c in range(4)] for t in range(2)]

        values = [fetch(first + i) for i in range(-1, count + 1)]
        for i in range(count):
            low, cur, high = values[i], values[i + 1], values[i + 2]
            across = [[low[t][c] + high[t][c] for c in range(4)] for t in range(2)]
            results = relax(cur, across, first + i, tiles, coef)
            for t, result in zip(tiles, results):
                for c in range(4):
                    put(level, final, t, c, first + i, result[c])

    def sweep_inside(level, final):
        tiles = (0, 1) if level < SWEEPS - 1 else (0,)
        first, last = level + 1, layers - 2 - level
        total = last - first + 1
        trips = 2
        chunk = total // trips

        def step(k, carry):
            sweep_run(level, first + k * chunk, chunk, tiles, final)
            return carry

        lax.fori_loop(0, trips, step, 0)

    def sweep_end(level, ghosts, at_start, final):
        tiles = (0, 1) if level < SWEEPS - 1 else (0,)
        src = level % 2
        count = level + 1
        span = range(0, count) if at_start else range(layers - count, layers)

        def fetch(layer):
            if layer < 0 or layer >= layers:
                return ghosts
            return [[buffers[t][src, c, layer] for c in range(4)] for t in range(2)]

        values = {layer: fetch(layer) for layer in range(span[0] - 1, span[-1] + 2)}
        for layer in span:
            low, cur, high = values[layer - 1], values[layer], values[layer + 1]
            across = [[low[t][c] + high[t][c] for c in range(4)] for t in range(2)]
            results = relax(cur, across, layer, tiles, coef)
            for t, result in zip(tiles, results):
                for c in range(4):
                    put(level, final, t, c, layer, result[c])

    def next_sweep(level, span, ghosts):
        tiles = (0, 1) if level < SWEEPS - 1 else (0,)
        src, dst = level % 2, (level + 1) % 2

        def fetch(layer):
            if layer < 0:
                return ghosts
            return [[nxt[src, t, c, layer] for c in range(4)] for t in range(2)]

        values = {layer: fetch(layer) for layer in range(span[0] - 1, span[-1] + 2)}
        for layer in span:
            low, cur, high = values[layer - 1], values[layer], values[layer + 1]
            across = [[low[t][c] + high[t][c] for c in range(4)] for t in range(2)]
            for t, result in zip(tiles, relax(cur, across, layer, tiles, nxt_coef)):
                for c in range(4):
                    nxt[dst, t, c, layer] = result[c]

    def coefficients_of(tile, mask=None, read=None):
        def step(layer, carry):
            lab = read(layer)
            rr, ri = look(real_table, lab), look(imag_table, lab)
            if mask is not None:
                rr, ri = rr * mask, ri * mask
            coef[0, tile, layer] = rr
            coef[1, tile, layer] = ri
            coef[4, tile, layer] = look(weight_table, lab)
            return carry

        lax.fori_loop(0, layers, step, 0, unroll=4)

    pl.semaphore_wait(barrier, len(greeted))
    loads[1].wait()
    trace_copy().start()
    next_copies()[0].start()
    for load in loads[2:4]:
        load.wait()
    loads[4].start()
    for c in range(4):
        pack_halo(0, c, lambda l, c=c: own[0, c, l])
    for copy in halo_copies(0):
        copy.start()
    pack_halo(0, 4, lambda l: coef[2, 0, l])
    pack_halo(0, 5, lambda l: coef[3, 0, l])
    pack_halo(0, 6, lambda l: labels[l].astype(F32))
    for load in small_loads:
        load.wait()

    wave = jnp.zeros((8, 128), F32)
    absorb = jnp.zeros((8, 128), F32)
    weight_table = jnp.zeros((8, 128), F32)
    for m in range(16):
        wave = jnp.where(lane == m, wave_s[m], wave)
        absorb = jnp.where(lane == m, absorb_s[m], absorb)
        weight_table = jnp.where(lane == m, design_s[m], weight_table)
    shifted = 6.0 - wave
    modulus = shifted * shifted + absorb * absorb
    real_table = shifted / modulus
    imag_table = absorb / modulus

    def look(table, index):
        return jnp.take_along_axis(table, index, axis=1, mode="promise_in_bounds")

    position = row * 128 + lane

    def place(step, carry):
        for t in range(16):
            point = step * 16 + t
            carry = jnp.where(position == pairs_s[0, point], point, carry)
        return carry

    loads[0].wait()
    pairs = pairs_v[...]

    def gather_points(read_row, index):
        index_row = lax.shift_right_logical(index, 7)
        index_lane = lax.bitwise_and(index, 127)
        out = jnp.zeros((8, 128), F32)
        for r in range(8):
            source_row = jnp.broadcast_to(read_row(r), (8, 128))
            out = jnp.where(index_row == r, look(source_row, index_lane), out)
        return out

    def left_ghosts(it):
        return [[left_in[it, t, c] * not_first for c in range(4)] for t in range(2)]

    for it in range(ITERS):
        outgoing[it, 0] = jnp.zeros((32, 128), BF16)
        outgoing[it, n_sub + 1] = jnp.zeros((32, 128), BF16)

    for it in range(ITERS):
        if it == 0:
            trace_copy().wait_recv()
        facing = []
        for c in range(4):
            taken = gather_points(
                lambda r: (facing_in[c] if it == 0 else nxt[0, 0, c, 0])[r : r + 1, :], pairs
            )
            taken = taken * not_last
            facing.append(taken)
            face[1, c] = taken
            rows32[0, pl.ds(c, 8, stride=4), :] = taken - own[0, c, layers - 1]
        jumps[it, 0] = rows32[0].astype(BF16)
        for slot in order:
            jump_copy(it, slot).start()
        for t in range(2):
            last = [own[0, 2 * t + k, layers - 1] for k in range(2)]
            side_out[it, 16 * t : 16 * t + 16] = jnp.concatenate(last, 0).astype(BF16)
            side_out[it, 32 + 16 * t : 48 + 16 * t] = jnp.concatenate(
                facing[2 * t : 2 * t + 2], 0
            ).astype(BF16)
        for copy in side_copies(it):
            copy.start()

        if it == 0:
            for copy in halo_copies(0, True):
                copy.start()
            coefficients_of(0, read=lambda l: labels[l])
            next_copies()[1].start()
            inverse = lax.fori_loop(0, 64, place, jnp.zeros((8, 128), jnp.int32))
            inv_out[...] = inverse
            for copy in inverse_copies():
                copy.start()
            loads[4].wait()

            def turn(k, carry):
                rows = pl.ds(pl.multiple_of(128 * k, 128), 128)
                for h in range(2):
                    turned_block[h, :, rows] = jnp.transpose(block[h, rows, :])
                return carry

            lax.fori_loop(0, block.shape[1] // 128, turn, 0)
        else:
            ghost_copy(0).wait_recv()
            for level in range(SWEEPS):
                sweep_end(level, left_ghosts(0), True, False)
            for c in range(4):
                pack_halo(it, c, lambda l, c=c: own[0, c, l], 0, 2)
            for copy in halo_copies(it, True):
                copy.start()
            all_halos(it).wait_recv()
            unpack_fields(it, 2, half // 2)
        contract = (((1,), (0,)), ((), ()))
        width = block.shape[1] // 2

        def product(columns):
            return lax.dot_general(
                stacked[0], turned_block[0, :, columns], contract, preferred_element_type=F32
            ) + lax.dot_general(
                stacked[1], turned_block[1, :, columns], contract, preferred_element_type=F32
            )

        if it == 0:
            trace_copy().wait_send()
        all_jumps(it).wait_recv()
        for i in range(0, n_sub, 4):
            first = [jumps[it, i + t].astype(F32) for t in range(4)]
            for r in range(8):
                k, odd = r // 2, r % 2
                plain, turned = [], []
                for t in (0, 2):
                    a = first[t][8 * k : 8 * k + 8]
                    b = first[t + 1][8 * k : 8 * k + 8]
                    v = jnp.where(upper, roll4(a) if odd else a, b if odd else roll4(b))
                    plain.append(v)
                    turned.append(jnp.where(even, -pltpu.roll(v, 7, 0), pltpu.roll(v, 1, 0)))
                columns = pl.ds(r * 128, 128)
                rows = pl.ds(4 * i, 16)
                stacked[0, rows, columns] = jnp.concatenate(plain, 0).astype(BF16)
                stacked[1, rows, columns] = jnp.concatenate(turned, 0).astype(BF16)
        for part in range(2):
            total = product(pl.ds(width * part, width))
            here = slice(16 * part, 16 * part + 16)
            for i in range(0, n_sub, 2):
                rows = total[4 * i : 4 * i + 8]
                evens, odds = [], []
                for k in range(2):
                    a = rows[:, 256 * k : 256 * k + 128]
                    b = rows[:, 256 * k + 128 : 256 * k + 256]
                    evens.append(jnp.where(upper, a, roll4(b)))
                    odds.append(jnp.where(upper, roll4(a), b))
                outgoing[it, source_of(i) + 1, here] = jnp.concatenate(evens, 0).astype(BF16)
                outgoing[it, source_of(i + 1) + 1, here] = jnp.concatenate(odds, 0).astype(BF16)
        for slot in order:
            product_copy(it, slot).start()
        for k in range(3):
            products[it, 0, k] = outgoing[it, me_s + k]

        if it == 0:
            all_halos(it, True).wait_recv()
            all_halos(it).wait_recv()
            unpack_fields(it, 0, half // 2)
            for c in range(2):
                def write_source(l, v, c=c):
                    coef[2 + c, 1, l] = v

                unpack_halo(0, 4 + c, write_source)

            def write_coef(l, v):
                lab = v.astype(jnp.int32)
                coef[0, 1, l] = look(real_table, lab) * beside_mask
                coef[1, 1, l] = look(imag_table, lab) * beside_mask
                coef[4, 1, l] = look(weight_table, lab)

            unpack_halo(0, 6, write_coef)
            for c in range(4):
                for layer in range(depth):
                    nxt_out[c, layer] = beside[0, c, layer]
            for copy in next_copies()[2:]:
                copy.start()
        else:
            all_halos(it, True).wait_recv()
            unpack_fields(it, 0, 2)
        final = it == ITERS - 1
        for level in range(SWEEPS):
            sweep_inside(level, final)
        if not final:
            for c in range(4):
                pack_halo(it + 1, c, lambda l, c=c: own[0, c, l], 2)
            for copy in halo_copies(it + 1):
                copy.start()

        if not final:
            for copy in next_copies():
                copy.wait_recv()
            next_sweep(0, range(1, depth - 1), None)
            next_sweep(1, range(2, depth - 2), None)
            all_inverses().wait_recv()
            inverse_beside = jnp.where(upper, inv_in[1], inv_in[0])
        all_sides(it).wait_recv()
        all_products(it).wait_recv()
        for k in range(3):
            owner = owner_s[0, lax.rem(me_s + n_sub + k - 1, n_sub)]
            rows32[k] = products[it, slot_of(owner), k].astype(F32)
        right = [[], []]
        for c in range(4):
            moved = [rows32[k, pl.ds(c, 8, stride=4), :] for k in range(3)]
            pair = pl.ds(16 * (c // 2), 16)
            half_rows = slice(8 * (c % 2), 8 * (c % 2) + 8)
            lasts = [side_in[it, k, pair].astype(F32)[half_rows] for k in range(2)]
            pair = pl.ds(32 + 16 * (c // 2), 16)
            faces = [side_in[it, k, pair].astype(F32)[half_rows] for k in range(2)]
            right[0].append((face[1, c] + moved[1]) * not_last)
            right[1].append(
                jnp.where(upper, faces[1] + moved[2], faces[0] + moved[0]) * not_last
            )
            face[1, c] = own[0, c, layers - 1] - moved[1]
            face[0, c] = lasts[0] - moved[0]
            face[2, c] = lasts[1] - moved[2]
        left = [[], []]
        for c in range(4):
            left[0].append(gather_points(lambda r: face[1, c, r : r + 1, :], inverse))
            left[1].append(
                gather_points(
                    lambda r: jnp.where(
                        upper,
                        jnp.broadcast_to(face[2, c, r : r + 1, :], (8, 128)),
                        jnp.broadcast_to(face[0, c, r : r + 1, :], (8, 128)),
                    ),
                    inverse_beside,
                )
            )
            left_out[it, 0, c] = left[0][c]
            left_out[it, 1, c] = left[1][c]
        ghost_copy(it).start()
        if not final:
            for level in range(SWEEPS):
                next_sweep(level, ((0,), (0, 1), (0, 1), (0,))[level], left)
                sweep_end(level, right, False, final)
        else:
            for copy in next_copies():
                copy.wait_send()
            for k in range(ITERS):
                for copy in (
                    all_jumps(k),
                    all_products(k),
                    all_sides(k),
                    all_halos(k),
                    all_halos(k, True),
                ):
                    copy.wait_send()
            all_inverses().wait_send()
            ghost_copy(0).wait_send()
            for level in range(SWEEPS):
                sweep_end(level, right, False, final)
            ghost_copy(it).wait_recv()
            left = left_ghosts(it)
            for level in range(SWEEPS):
                sweep_end(level, left, True, final)
            ghost_copy(it).wait_send()


def store_kernel(forward_v, adjoint_v, forward_h, adjoint_h, sem):
    copies = [
        pltpu.make_async_copy(forward_v, forward_h, sem.at[0]),
        pltpu.make_async_copy(adjoint_v, adjoint_h, sem.at[1]),
    ]
    for copy in copies:
        copy.start()
    for copy in copies:
        copy.wait()


def solution(mesh):
    n_dom, n_sub = mesh.shape["dom"], mesh.shape["sub"]
    nx = 4 if n_sub % 4 == 0 and n_sub > 4 else 2

    def per_device(
        start_fields,
        source,
        labels,
        wavenumber2,
        absorption,
        design_weight,
        pairs,
        block_index,
        blocks,
    ):
        layers = labels.shape[0]
        points = pairs.shape[-1]
        slots = n_sub
        hbm = pl.BlockSpec(memory_space=pltpu.HBM)
        vmem = pl.BlockSpec(memory_space=pltpu.VMEM)
        out = jax.ShapeDtypeStruct((2,) + labels.shape, F32)
        dma = pltpu.SemaphoreType.DMA
        operands = [
            pltpu.with_memory_space_constraint(operand, pltpu.HBM)
            for operand in (
                pairs[0],
                block_index,
                wavenumber2,
                absorption,
                design_weight,
                pairs.reshape(8, 128),
                start_fields,
                source,
                labels,
                blocks,
            )
        ]
        results = pl.pallas_call(
            functools.partial(kernel, (n_dom, n_sub, nx)),
            out_shape=(out, out),
            in_specs=[hbm] * 10,
            out_specs=(vmem, vmem),
            scratch_shapes=[
                pltpu.SMEM((1, points), jnp.int32),
                pltpu.SMEM(block_index.shape, jnp.int32),
                pltpu.SMEM(wavenumber2.shape, F32),
                pltpu.SMEM(absorption.shape, F32),
                pltpu.SMEM(design_weight.shape, F32),
                pltpu.VMEM((8, 128), jnp.int32),
                pltpu.VMEM((2, 4, layers, 8, 128), F32),
                pltpu.VMEM((2, 4, layers, 8, 128), F32),
                pltpu.VMEM((5, 2, layers, 8, 128), F32),
                pltpu.VMEM((layers, 8, 128), jnp.int32),
                pltpu.VMEM((2, points, points), BF16),
                pltpu.VMEM((2, points, points), BF16),
                pltpu.VMEM((4, 8, 128), F32),
                pltpu.VMEM((ITERS, slots, 32, 128), BF16),
                pltpu.VMEM((2, 4 * slots, points), BF16),
                pltpu.VMEM((ITERS, slots + 2, 32, 128), BF16),
                pltpu.VMEM((ITERS, slots, 3, 32, 128), BF16),
                pltpu.VMEM((3, 32, 128), F32),
                pltpu.VMEM((3, 4, 8, 128), F32),
                pltpu.VMEM((ITERS, 2, 4, 8, 128), F32),
                pltpu.VMEM((ITERS, 2, 4, 8, 128), F32),
                pltpu.VMEM((ITERS, 64, 128), BF16),
                pltpu.VMEM((ITERS, 2, 64, 128), BF16),
                pltpu.VMEM((8, 128), jnp.int32),
                pltpu.VMEM((2, 8, 128), jnp.int32),
                pltpu.VMEM((4, 7, layers // 4, 16, 128), BF16),
                pltpu.VMEM((4, 7, layers // 4, 16, 128), BF16),
                dma((10,)),
                dma((2,)),
                dma((ITERS,)),
                dma((ITERS,)),
                dma((ITERS,)),
                dma((ITERS,)),
                dma((ITERS,)),
                dma((ITERS,)),
                dma((ITERS,)),
                dma((ITERS,)),
                dma(()),
                dma(()),
                dma((2 * ITERS,)),
                dma((2 * ITERS,)),
                pltpu.VMEM((2, 2, 4, SWEEPS + 1, 8, 128), F32),
                pltpu.VMEM((5, 2, SWEEPS, 8, 128), F32),
                pltpu.VMEM((4, SWEEPS + 1, 8, 128), F32),
                dma((4,)),
                dma((4,)),
            ],
            compiler_params=pltpu.CompilerParams(
                collective_id=0, has_side_effects=True, vmem_limit_bytes=20 * 1024 * 1024
            ),
        )(*operands)
        return pl.pallas_call(
            store_kernel,
            out_shape=(out, out),
            in_specs=[vmem, vmem],
            out_specs=(hbm, hbm),
            scratch_shapes=[dma((2,))],
            compiler_params=pltpu.CompilerParams(vmem_limit_bytes=4 * 1024 * 1024),
        )(*results)

    placed = (
        P(None, "dom", "sub", None),
        P(None, "dom", "sub", None),
        P("dom", "sub", None),
        P(),
        P(),
        P(),
        P("dom", "sub", None),
        P("dom", None),
        P("dom", "sub", None, None, None),
    )
    return jax.shard_map(
        per_device,
        mesh=mesh,
        in_specs=placed,
        out_specs=(P(None, "dom", "sub", None), P(None, "dom", "sub", None)),
        check_vma=False,
    )
```

```python
import functools

import jax
import jax.numpy as jnp
from jax import lax
from jax.experimental import pallas as pl
from jax.experimental.pallas import tpu as pltpu
from jax.sharding import PartitionSpec as P

SWEEPS = 4
ITERS = 2
MESH = pl.DeviceIdType.MESH
F32 = jnp.float32
BF16 = jnp.bfloat16


def torus_offsets(nx, ny):
    offsets = [(dx, dy) for dy in range(ny) for dx in range(nx)]
    hops = lambda o: min(o[0], nx - o[0]) + min(o[1], ny - o[1])
    order = sorted(range(1, nx * ny), key=lambda i: -hops(offsets[i]))
    return offsets, order


def kernel(
    shape,
    pairs_flat_h,
    owner_h,
    wave_h,
    absorb_h,
    design_h,
    pairs_h,
    fields_h,
    source_h,
    labels_h,
    blocks_h,
    forward,
    adjoint,
    pairs_s,
    owner_s,
    wave_s,
    absorb_s,
    design_s,
    pairs_v,
    own,
    beside,
    coef,
    labels,
    block,
    turned_block,
    facing_in,
    jumps,
    stacked,
    outgoing,
    products,
    rows32,
    face,
    left_out,
    left_in,
    side_out,
    side_in,
    inv_out,
    inv_in,
    halo_out,
    halo_in,
    load_sem,
    trace_sem,
    jump_send,
    jump_recv,
    prod_send,
    prod_recv,
    ghost_send,
    ghost_recv,
    side_send,
    side_recv,
    inv_send,
    inv_recv,
    halo_send,
    halo_recv,
    nxt,
    nxt_coef,
    nxt_out,
    nxt_send,
    nxt_recv,
):
    n_dom, n_sub, nx = shape
    ny = n_sub // nx
    layers = fields_h.shape[1]
    offsets, order = torus_offsets(nx, ny)
    me_d = lax.axis_index("dom")
    me_s = lax.axis_index("sub")
    my_x, my_y = lax.rem(me_s, nx), lax.div(me_s, nx)
    before_d, after_d = lax.rem(me_d + n_dom - 1, n_dom), lax.rem(me_d + 1, n_dom)
    before_s, after_s = lax.rem(me_s + n_sub - 1, n_sub), lax.rem(me_s + 1, n_sub)

    def member(slot):
        dx, dy = offsets[slot]
        return lax.rem(my_y + dy, ny) * nx + lax.rem(my_x + dx, nx)

    barrier = pltpu.get_barrier_semaphore()
    greeted = [(me_d, member(slot)) for slot in reversed(order)]
    greeted = [(before_d, me_s), (after_d, me_s)] + greeted
    for device in greeted:
        pl.semaphore_signal(barrier, inc=1, device_id=device, device_id_type=MESH)

    small_loads = [
        pltpu.make_async_copy(src, dst, load_sem.at[5 + k])
        for k, (src, dst) in enumerate(
            (
                (pairs_flat_h, pairs_s),
                (owner_h, owner_s),
                (wave_h, wave_s),
                (absorb_h, absorb_s),
                (design_h, design_s),
            )
        )
    ]
    for load in small_loads:
        load.start()
    loads = [
        pltpu.make_async_copy(pairs_h, pairs_v, load_sem.at[0]),
        pltpu.make_async_copy(fields_h, own.at[0], load_sem.at[1]),
        pltpu.make_async_copy(labels_h, labels, load_sem.at[2]),
        pltpu.make_async_copy(source_h, coef.at[2:4, 0], load_sem.at[3]),
        pltpu.make_async_copy(blocks_h.at[0, 0], block, load_sem.at[4]),
    ]
    for load in loads[:4]:
        load.start()

    row = lax.broadcasted_iota(jnp.int32, (8, 128), 0)
    lane = lax.broadcasted_iota(jnp.int32, (8, 128), 1)
    upper = row < 4
    even = lax.rem(row, 2) == 0
    not_first = jnp.where(me_d == 0, 0.0, 1.0).astype(F32)
    not_last = jnp.where(me_d == n_dom - 1, 0.0, 1.0).astype(F32)
    has_before = jnp.where(me_s == 0, 0.0, 1.0).astype(F32)
    has_after = jnp.where(me_s == n_sub - 1, 0.0, 1.0).astype(F32)
    beside_mask = jnp.where(upper, has_after, has_before)

    def roll4(value):
        return pltpu.roll(value, 4, 0)

    depth = nxt.shape[3]

    def trace_copy():
        return pltpu.make_async_remote_copy(
            src_ref=own.at[0, :, 0],
            dst_ref=facing_in,
            send_sem=trace_sem.at[0],
            recv_sem=trace_sem.at[1],
            device_id=(before_d, me_s),
            device_id_type=MESH,
        )

    def next_copies():
        copies = []
        for k, (src, dst) in enumerate(
            (
                (fields_h.at[:, 0:depth], nxt.at[0, 0]),
                (coef.at[:, 0, 0 : depth - 1], nxt_coef.at[:, 0]),
                (nxt_out, nxt.at[0, 1]),
                (coef.at[:, 1, 0 : depth - 1], nxt_coef.at[:, 1]),
            )
        ):
            copies.append(
                pltpu.make_async_remote_copy(
                    src_ref=src,
                    dst_ref=dst,
                    send_sem=nxt_send.at[k % 2],
                    recv_sem=nxt_recv.at[k % 2],
                    device_id=(before_d, me_s),
                    device_id_type=MESH,
                )
            )
        return copies

    def source_of(slot):
        dx, dy = offsets[slot]
        return lax.rem(my_y + ny - dy, ny) * nx + lax.rem(my_x + nx - dx, nx)

    def slot_of(member_index):
        dx = lax.rem(lax.rem(member_index, nx) - my_x + nx, nx)
        dy = lax.rem(lax.div(member_index, nx) - my_y + ny, ny)
        return dy * nx + dx

    def jump_copy(it, slot):
        return pltpu.make_async_remote_copy(
            src_ref=jumps.at[it, 0],
            dst_ref=jumps.at[it, slot],
            send_sem=jump_send.at[it],
            recv_sem=jump_recv.at[it],
            device_id=(me_d, member(slot)),
            device_id_type=MESH,
        )

    def product_copy(it, slot):
        back = source_of(slot)
        return pltpu.make_async_remote_copy(
            src_ref=outgoing.at[it, pl.ds(back, 3)],
            dst_ref=products.at[it, slot],
            send_sem=prod_send.at[it],
            recv_sem=prod_recv.at[it],
            device_id=(me_d, back),
            device_id_type=MESH,
        )

    def all_of(ref, send_sem, recv_sem):
        return pltpu.make_async_remote_copy(
            src_ref=ref,
            dst_ref=ref,
            send_sem=send_sem,
            recv_sem=recv_sem,
            device_id=(me_d, after_s),
            device_id_type=MESH,
        )

    others = pl.ds(1, n_sub - 1)

    def all_jumps(it):
        return all_of(jumps.at[it, others], jump_send.at[it], jump_recv.at[it])

    def all_products(it):
        return all_of(products.at[it, others], prod_send.at[it], prod_recv.at[it])

    def all_sides(it):
        return all_of(side_in.at[it], side_send.at[it], side_recv.at[it])

    def all_next():
        return [
            all_of(nxt.at[0], nxt_send.at[0], nxt_recv.at[0]),
            all_of(nxt_coef, nxt_send.at[1], nxt_recv.at[1]),
        ]

    def all_inverses():
        return all_of(inv_in, inv_send, inv_recv)

    def ghost_copy(it):
        return pltpu.make_async_remote_copy(
            src_ref=left_out.at[it],
            dst_ref=left_in.at[it],
            send_sem=ghost_send.at[it],
            recv_sem=ghost_recv.at[it],
            device_id=(after_d, me_s),
            device_id_type=MESH,
        )

    def beside_copies(src, dst, send_sem, recv_sem):
        return [
            pltpu.make_async_remote_copy(
                src_ref=src,
                dst_ref=dst.at[k],
                send_sem=send_sem,
                recv_sem=recv_sem,
                device_id=(me_d, sub),
                device_id_type=MESH,
            )
            for k, sub in enumerate((after_s, before_s))
        ]

    def side_copies(it):
        return beside_copies(side_out.at[it], side_in.at[it], side_send.at[it], side_recv.at[it])

    def inverse_copies():
        return beside_copies(inv_out, inv_in, inv_send, inv_recv)

    def halo_part(it, second):
        groups = halo_out.shape[2]
        if it == 0:
            return (pl.ds(4, 3) if second else pl.ds(0, 4)), pl.ds(0, groups)
        return pl.ds(0, 4), (pl.ds(0, 2) if second else pl.ds(2, groups - 2))

    def halo_copies(it, second=False):
        copies = []
        for k, sub in enumerate((after_s, before_s)):
            part = (2 * it + k,) + halo_part(it, second)
            copies.append(
                pltpu.make_async_remote_copy(
                    src_ref=halo_out.at[part],
                    dst_ref=halo_in.at[part],
                    send_sem=halo_send.at[it * (1 + second)],
                    recv_sem=halo_recv.at[it * (1 + second)],
                    device_id=(me_d, sub),
                    device_id_type=MESH,
                )
            )
        return copies

    def all_halos(it, second=False):
        rest = halo_part(it, second) if it else (pl.ds(0, halo_in.shape[1]), pl.ds(0, halo_in.shape[2]))
        k = it * (1 + second)
        return all_of(halo_in.at[(pl.ds(2 * it, 2),) + rest], halo_send.at[k], halo_recv.at[k])

    half = layers // 2

    def pack_halo(it, item, read, start=0, stop=None):
        base = 2 * it

        def step(k, carry):
            downs, ups = [], []
            for t in range(2):
                near = read(2 * k + t)
                far = roll4(read(layers - 1 - 2 * k - t))
                downs.append(jnp.where(upper, far, near))
                ups.append(jnp.where(upper, near, far))
            halo_out[base, item, k] = jnp.concatenate(downs, 0).astype(BF16)
            halo_out[base + 1, item, k] = jnp.concatenate(ups, 0).astype(BF16)
            return carry

        lax.fori_loop(start, stop or half // 2, step, 0, unroll=2)

    def unpack_halo(it, item, write, start=0, stop=None):
        base = 2 * it

        def step(k, carry):
            down = halo_in[base, item, k].astype(F32)
            up = halo_in[base + 1, item, k].astype(F32)
            for t in range(2):
                d, u = down[8 * t : 8 * t + 8], up[8 * t : 8 * t + 8]
                write(2 * k + t, jnp.where(upper, u, d))
                write(layers - 1 - 2 * k - t, roll4(jnp.where(upper, d, u)))
            return carry

        lax.fori_loop(start, stop or half // 2, step, 0, unroll=2)

    def unpack_fields(it, start, stop):
        for c in range(4):
            def write_field(l, v, c=c):
                beside[0, c, l] = v * beside_mask

            unpack_halo(it, c, write_field, start, stop)

    def z_sum(v):
        low = jnp.where(lane == 0, 0.0, pltpu.roll(v, 1, 1))
        high = jnp.where(lane == 127, 0.0, pltpu.roll(v, 127, 1))
        return low + high

    def relax(cur, across, layer, tiles, table):
        sums = [[None] * 4 for _ in range(2)]
        for c in range(4):
            a, b = cur[0][c], cur[1][c]
            a_up, b_up = pltpu.roll(a, 1, 0), pltpu.roll(b, 1, 0)
            a_dn, b_dn = pltpu.roll(a, 7, 0), pltpu.roll(b, 7, 0)
            for t in tiles:
                v = (a, b)[t]
                mine_up, mine_dn = ((a_up, a_dn), (b_up, b_dn))[t]
                other_up, other_dn = ((b_up, b_dn), (a_up, a_dn))[t]
                y_sum = jnp.where(row == 0, other_up, mine_up) + jnp.where(
                    row == 7, other_dn, mine_dn
                )
                sums[t][c] = across[t][c] + y_sum + z_sum(v)
        results = []
        for t in tiles:
            rr, ri = table[0, t, layer], table[1, t, layer]
            w = table[4, t, layer]
            fr = table[2, t, layer] + sums[t][0]
            fi = table[3, t, layer] + sums[t][1]
            ar = w * cur[t][0] + sums[t][2]
            ai = w * cur[t][1] + sums[t][3]
            results.append(
                (rr * fr - ri * fi, rr * fi + ri * fr, rr * ar + ri * ai, rr * ai - ri * ar)
            )
        return results

    buffers = (own, beside)

    def put(level, final, t, c, layer, value):
        if final and level == SWEEPS - 1:
            (forward, adjoint)[c // 2][c % 2, layer] = value
        else:
            buffers[t][(level + 1) % 2, c, layer] = value

    def sweep_run(level, first, count, tiles, final):
        src = level % 2

        def fetch(layer):
            return [[buffers[t][src, c, layer] for c in range(4)] for t in range(2)]

        values = [fetch(first + i) for i in range(-1, count + 1)]
        for i in range(count):
            low, cur, high = values[i], values[i + 1], values[i + 2]
            across = [[low[t][c] + high[t][c] for c in range(4)] for t in range(2)]
            results = relax(cur, across, first + i, tiles, coef)
            for t, result in zip(tiles, results):
                for c in range(4):
                    put(level, final, t, c, first + i, result[c])

    def sweep_inside(level, final):
        tiles = (0, 1) if level < SWEEPS - 1 else (0,)
        first, last = level + 1, layers - 2 - level
        total = last - first + 1
        trips = 2
        chunk = total // trips

        def step(k, carry):
            sweep_run(level, first + k * chunk, chunk, tiles, final)
            return carry

        lax.fori_loop(0, trips, step, 0)

    def sweep_end(level, ghosts, at_start, final):
        tiles = (0, 1) if level < SWEEPS - 1 else (0,)
        src = level % 2
        count = level + 1
        span = range(0, count) if at_start else range(layers - count, layers)

        def fetch(layer):
            if layer < 0 or layer >= layers:
                return ghosts
            return [[buffers[t][src, c, layer] for c in range(4)] for t in range(2)]

        values = {layer: fetch(layer) for layer in range(span[0] - 1, span[-1] + 2)}
        for layer in span:
            low, cur, high = values[layer - 1], values[layer], values[layer + 1]
            across = [[low[t][c] + high[t][c] for c in range(4)] for t in range(2)]
            results = relax(cur, across, layer, tiles, coef)
            for t, result in zip(tiles, results):
                for c in range(4):
                    put(level, final, t, c, layer, result[c])

    def next_sweep(level, span, ghosts):
        tiles = (0, 1) if level < SWEEPS - 1 else (0,)
        src, dst = level % 2, (level + 1) % 2

        def fetch(layer):
            if layer < 0:
                return ghosts
            return [[nxt[src, t, c, layer] for c in range(4)] for t in range(2)]

        values = {layer: fetch(layer) for layer in range(span[0] - 1, span[-1] + 2)}
        for layer in span:
            low, cur, high = values[layer - 1], values[layer], values[layer + 1]
            across = [[low[t][c] + high[t][c] for c in range(4)] for t in range(2)]
            for t, result in zip(tiles, relax(cur, across, layer, tiles, nxt_coef)):
                for c in range(4):
                    nxt[dst, t, c, layer] = result[c]

    def coefficients_of(tile, mask=None, read=None):
        def step(layer, carry):
            lab = read(layer)
            rr, ri = look(real_table, lab), look(imag_table, lab)
            if mask is not None:
                rr, ri = rr * mask, ri * mask
            coef[0, tile, layer] = rr
            coef[1, tile, layer] = ri
            coef[4, tile, layer] = look(weight_table, lab)
            return carry

        lax.fori_loop(0, layers, step, 0, unroll=4)

    pl.semaphore_wait(barrier, len(greeted))
    loads[1].wait()
    trace_copy().start()
    next_copies()[0].start()
    for load in loads[2:4]:
        load.wait()
    loads[4].start()
    for c in range(4):
        pack_halo(0, c, lambda l, c=c: own[0, c, l])
    for copy in halo_copies(0):
        copy.start()
    pack_halo(0, 4, lambda l: coef[2, 0, l])
    pack_halo(0, 5, lambda l: coef[3, 0, l])
    pack_halo(0, 6, lambda l: labels[l].astype(F32))
    for load in small_loads:
        load.wait()

    wave = jnp.zeros((8, 128), F32)
    absorb = jnp.zeros((8, 128), F32)
    weight_table = jnp.zeros((8, 128), F32)
    for m in range(16):
        wave = jnp.where(lane == m, wave_s[m], wave)
        absorb = jnp.where(lane == m, absorb_s[m], absorb)
        weight_table = jnp.where(lane == m, design_s[m], weight_table)
    shifted = 6.0 - wave
    modulus = shifted * shifted + absorb * absorb
    real_table = shifted / modulus
    imag_table = absorb / modulus

    def look(table, index):
        return jnp.take_along_axis(table, index, axis=1, mode="promise_in_bounds")

    position = row * 128 + lane

    def place(step, carry):
        for t in range(16):
            point = step * 16 + t
            carry = jnp.where(position == pairs_s[0, point], point, carry)
        return carry

    loads[0].wait()
    pairs = pairs_v[...]

    def gather_points(read_row, index):
        index_row = lax.shift_right_logical(index, 7)
        index_lane = lax.bitwise_and(index, 127)
        out = jnp.zeros((8, 128), F32)
        for r in range(8):
            source_row = jnp.broadcast_to(read_row(r), (8, 128))
            out = jnp.where(index_row == r, look(source_row, index_lane), out)
        return out

    def left_ghosts(it):
        return [[left_in[it, t, c] * not_first for c in range(4)] for t in range(2)]

    for it in range(ITERS):
        outgoing[it, 0] = jnp.zeros((32, 128), BF16)
        outgoing[it, n_sub + 1] = jnp.zeros((32, 128), BF16)

    for it in range(ITERS):
        if it == 0:
            trace_copy().wait_recv()
        facing = []
        for c in range(4):
            taken = gather_points(
                lambda r: (facing_in[c] if it == 0 else nxt[0, 0, c, 0])[r : r + 1, :], pairs
            )
            taken = taken * not_last
            facing.append(taken)
            face[1, c] = taken
            rows32[0, pl.ds(c, 8, stride=4), :] = taken - own[0, c, layers - 1]
        jumps[it, 0] = rows32[0].astype(BF16)
        for slot in order:
            jump_copy(it, slot).start()
        for t in range(2):
            last = [own[0, 2 * t + k, layers - 1] for k in range(2)]
            side_out[it, 16 * t : 16 * t + 16] = jnp.concatenate(last, 0).astype(BF16)
            side_out[it, 32 + 16 * t : 48 + 16 * t] = jnp.concatenate(
                facing[2 * t : 2 * t + 2], 0
            ).astype(BF16)
        for copy in side_copies(it):
            copy.start()

        if it == 0:
            for copy in halo_copies(0, True):
                copy.start()
            coefficients_of(0, read=lambda l: labels[l])
            next_copies()[1].start()
            inverse = lax.fori_loop(0, 64, place, jnp.zeros((8, 128), jnp.int32))
            inv_out[...] = inverse
            for copy in inverse_copies():
                copy.start()
            loads[4].wait()

            def turn(k, carry):
                rows = pl.ds(pl.multiple_of(128 * k, 128), 128)
                for h in range(2):
                    turned_block[h, :, rows] = jnp.transpose(block[h, rows, :])
                return carry

            lax.fori_loop(0, block.shape[1] // 128, turn, 0)
        else:
            ghost_copy(0).wait_recv()
            for level in range(SWEEPS):
                sweep_end(level, left_ghosts(0), True, False)
            for c in range(4):
                pack_halo(it, c, lambda l, c=c: own[0, c, l], 0, 2)
            for copy in halo_copies(it, True):
                copy.start()
            all_halos(it).wait_recv()
            unpack_fields(it, 2, half // 2)
        contract = (((1,), (0,)), ((), ()))
        width = block.shape[1] // 2

        def product(columns):
            return lax.dot_general(
                stacked[0], turned_block[0, :, columns], contract, preferred_element_type=F32
            ) + lax.dot_general(
                stacked[1], turned_block[1, :, columns], contract, preferred_element_type=F32
            )

        if it == 0:
            trace_copy().wait_send()
        all_jumps(it).wait_recv()
        for i in range(0, n_sub, 4):
            first = [jumps[it, i + t].astype(F32) for t in range(4)]
            for r in range(8):
                k, odd = r // 2, r % 2
                plain, turned = [], []
                for t in (0, 2):
                    a = first[t][8 * k : 8 * k + 8]
                    b = first[t + 1][8 * k : 8 * k + 8]
                    v = jnp.where(upper, roll4(a) if odd else a, b if odd else roll4(b))
                    plain.append(v)
                    turned.append(jnp.where(even, -pltpu.roll(v, 7, 0), pltpu.roll(v, 1, 0)))
                columns = pl.ds(r * 128, 128)
                rows = pl.ds(4 * i, 16)
                stacked[0, rows, columns] = jnp.concatenate(plain, 0).astype(BF16)
                stacked[1, rows, columns] = jnp.concatenate(turned, 0).astype(BF16)
        for part in range(2):
            total = product(pl.ds(width * part, width))
            here = slice(16 * part, 16 * part + 16)
            for i in range(0, n_sub, 2):
                rows = total[4 * i : 4 * i + 8]
                evens, odds = [], []
                for k in range(2):
                    a = rows[:, 256 * k : 256 * k + 128]
                    b = rows[:, 256 * k + 128 : 256 * k + 256]
                    evens.append(jnp.where(upper, a, roll4(b)))
                    odds.append(jnp.where(upper, roll4(a), b))
                outgoing[it, source_of(i) + 1, here] = jnp.concatenate(evens, 0).astype(BF16)
                outgoing[it, source_of(i + 1) + 1, here] = jnp.concatenate(odds, 0).astype(BF16)
        for slot in order:
            product_copy(it, slot).start()
        for k in range(3):
            products[it, 0, k] = outgoing[it, me_s + k]

        if it == 0:
            all_halos(it).wait_recv()
            unpack_fields(it, 0, half // 2)
            for c in range(2):
                def write_source(l, v, c=c):
                    coef[2 + c, 1, l] = v

                unpack_halo(0, 4 + c, write_source)

            def write_coef(l, v):
                lab = v.astype(jnp.int32)
                coef[0, 1, l] = look(real_table, lab) * beside_mask
                coef[1, 1, l] = look(imag_table, lab) * beside_mask
                coef[4, 1, l] = look(weight_table, lab)

            unpack_halo(0, 6, write_coef)
            for c in range(4):
                for layer in range(depth):
                    nxt_out[c, layer] = beside[0, c, layer]
            for copy in next_copies()[2:]:
                copy.start()
        else:
            all_halos(it, True).wait_recv()
            unpack_fields(it, 0, 2)
        final = it == ITERS - 1
        for level in range(SWEEPS):
            sweep_inside(level, final)
        if not final:
            for c in range(4):
                pack_halo(it + 1, c, lambda l, c=c: own[0, c, l], 2)
            for copy in halo_copies(it + 1):
                copy.start()

        if not final:
            for copy in all_next():
                copy.wait_recv()
            next_sweep(0, range(1, depth - 1), None)
            next_sweep(1, range(2, depth - 2), None)
            all_inverses().wait_recv()
            inverse_beside = jnp.where(upper, inv_in[1], inv_in[0])
        all_sides(it).wait_recv()
        all_products(it).wait_recv()
        for k in range(3):
            owner = owner_s[0, lax.rem(me_s + n_sub + k - 1, n_sub)]
            rows32[k] = products[it, slot_of(owner), k].astype(F32)
        right = [[], []]
        for c in range(4):
            moved = [rows32[k, pl.ds(c, 8, stride=4), :] for k in range(3)]
            pair = pl.ds(16 * (c // 2), 16)
            half_rows = slice(8 * (c % 2), 8 * (c % 2) + 8)
            lasts = [side_in[it, k, pair].astype(F32)[half_rows] for k in range(2)]
            pair = pl.ds(32 + 16 * (c // 2), 16)
            faces = [side_in[it, k, pair].astype(F32)[half_rows] for k in range(2)]
            right[0].append((face[1, c] + moved[1]) * not_last)
            right[1].append(
                jnp.where(upper, faces[1] + moved[2], faces[0] + moved[0]) * not_last
            )
            face[1, c] = own[0, c, layers - 1] - moved[1]
            face[0, c] = lasts[0] - moved[0]
            face[2, c] = lasts[1] - moved[2]
        left = [[], []]
        for c in range(4):
            left[0].append(gather_points(lambda r: face[1, c, r : r + 1, :], inverse))
            left[1].append(
                gather_points(
                    lambda r: jnp.where(
                        upper,
                        jnp.broadcast_to(face[2, c, r : r + 1, :], (8, 128)),
                        jnp.broadcast_to(face[0, c, r : r + 1, :], (8, 128)),
                    ),
                    inverse_beside,
                )
            )
            left_out[it, 0, c] = left[0][c]
            left_out[it, 1, c] = left[1][c]
        ghost_copy(it).start()
        if not final:
            for level in range(SWEEPS):
                next_sweep(level, ((0,), (0, 1), (0, 1), (0,))[level], left)
                sweep_end(level, right, False, final)
        else:
            for copy in all_next():
                copy.wait_send()
            for k in range(ITERS):
                for copy in (
                    all_jumps(k),
                    all_products(k),
                    all_sides(k),
                    all_halos(k),
                ):
                    copy.wait_send()
            all_halos(1, True).wait_send()
            all_inverses().wait_send()
            ghost_copy(0).wait_send()
            for level in range(SWEEPS):
                sweep_end(level, right, False, final)
            ghost_copy(it).wait_recv()
            left = left_ghosts(it)
            for level in range(SWEEPS):
                sweep_end(level, left, True, final)
            ghost_copy(it).wait_send()


def store_kernel(forward_v, adjoint_v, forward_h, adjoint_h, sem):
    copies = [
        pltpu.make_async_copy(forward_v, forward_h, sem.at[0]),
        pltpu.make_async_copy(adjoint_v, adjoint_h, sem.at[1]),
    ]
    for copy in copies:
        copy.start()
    for copy in copies:
        copy.wait()


def solution(mesh):
    n_dom, n_sub = mesh.shape["dom"], mesh.shape["sub"]
    nx = 4 if n_sub % 4 == 0 and n_sub > 4 else 2

    def per_device(
        start_fields,
        source,
        labels,
        wavenumber2,
        absorption,
        design_weight,
        pairs,
        block_index,
        blocks,
    ):
        layers = labels.shape[0]
        points = pairs.shape[-1]
        slots = n_sub
        hbm = pl.BlockSpec(memory_space=pltpu.HBM)
        vmem = pl.BlockSpec(memory_space=pltpu.VMEM)
        out = jax.ShapeDtypeStruct((2,) + labels.shape, F32)
        dma = pltpu.SemaphoreType.DMA
        operands = [
            pltpu.with_memory_space_constraint(operand, pltpu.HBM)
            for operand in (
                pairs[0],
                block_index,
                wavenumber2,
                absorption,
                design_weight,
                pairs.reshape(8, 128),
                start_fields,
                source,
                labels,
                blocks,
            )
        ]
        results = pl.pallas_call(
            functools.partial(kernel, (n_dom, n_sub, nx)),
            out_shape=(out, out),
            in_specs=[hbm] * 10,
            out_specs=(vmem, vmem),
            scratch_shapes=[
                pltpu.SMEM((1, points), jnp.int32),
                pltpu.SMEM(block_index.shape, jnp.int32),
                pltpu.SMEM(wavenumber2.shape, F32),
                pltpu.SMEM(absorption.shape, F32),
                pltpu.SMEM(design_weight.shape, F32),
                pltpu.VMEM((8, 128), jnp.int32),
                pltpu.VMEM((2, 4, layers, 8, 128), F32),
                pltpu.VMEM((2, 4, layers, 8, 128), F32),
                pltpu.VMEM((5, 2, layers, 8, 128), F32),
                pltpu.VMEM((layers, 8, 128), jnp.int32),
                pltpu.VMEM((2, points, points), BF16),
                pltpu.VMEM((2, points, points), BF16),
                pltpu.VMEM((4, 8, 128), F32),
                pltpu.VMEM((ITERS, slots, 32, 128), BF16),
                pltpu.VMEM((2, 4 * slots, points), BF16),
                pltpu.VMEM((ITERS, slots + 2, 32, 128), BF16),
                pltpu.VMEM((ITERS, slots, 3, 32, 128), BF16),
                pltpu.VMEM((3, 32, 128), F32),
                pltpu.VMEM((3, 4, 8, 128), F32),
                pltpu.VMEM((ITERS, 2, 4, 8, 128), F32),
                pltpu.VMEM((ITERS, 2, 4, 8, 128), F32),
                pltpu.VMEM((ITERS, 64, 128), BF16),
                pltpu.VMEM((ITERS, 2, 64, 128), BF16),
                pltpu.VMEM((8, 128), jnp.int32),
                pltpu.VMEM((2, 8, 128), jnp.int32),
                pltpu.VMEM((4, 7, layers // 4, 16, 128), BF16),
                pltpu.VMEM((4, 7, layers // 4, 16, 128), BF16),
                dma((10,)),
                dma((2,)),
                dma((ITERS,)),
                dma((ITERS,)),
                dma((ITERS,)),
                dma((ITERS,)),
                dma((ITERS,)),
                dma((ITERS,)),
                dma((ITERS,)),
                dma((ITERS,)),
                dma(()),
                dma(()),
                dma((3,)),
                dma((3,)),
                pltpu.VMEM((2, 2, 4, SWEEPS + 1, 8, 128), F32),
                pltpu.VMEM((5, 2, SWEEPS, 8, 128), F32),
                pltpu.VMEM((4, SWEEPS + 1, 8, 128), F32),
                dma((2,)),
                dma((2,)),
            ],
            compiler_params=pltpu.CompilerParams(
                collective_id=0, has_side_effects=True, vmem_limit_bytes=20 * 1024 * 1024
            ),
        )(*operands)
        return pl.pallas_call(
            store_kernel,
            out_shape=(out, out),
            in_specs=[vmem, vmem],
            out_specs=(hbm, hbm),
            scratch_shapes=[dma((2,))],
            compiler_params=pltpu.CompilerParams(vmem_limit_bytes=4 * 1024 * 1024),
        )(*results)

    placed = (
        P(None, "dom", "sub", None),
        P(None, "dom", "sub", None),
        P("dom", "sub", None),
        P(),
        P(),
        P(),
        P("dom", "sub", None),
        P("dom", None),
        P("dom", "sub", None, None, None),
    )
    return jax.shard_map(
        per_device,
        mesh=mesh,
        in_specs=placed,
        out_specs=(P(None, "dom", "sub", None), P(None, "dom", "sub", None)),
        check_vma=False,
    )
```
